128 devices in a mesh: gx: 4 (over z), gy: 32 (over x, y, core).
Axes of the slice: x: 4, y: 4, z: 4, core: 2. Of those that a mesh axis runs over, the one named last changes fastest.
Arguments:
- operator_blocks: bfloat16 [1024, 6, 256, 256], P(('gx', 'gy')), may hold values from -0.15625 to 0.15625
- local_columns: int32 [1024, 2], P(('gx', 'gy')), may hold values from 0 to 7
- remote_columns: int32 [1024, 4], P(('gx', 'gy')), may hold values from 8 to 41
- match_slots: int32 [1024, 6, 2], P(('gx', 'gy')), may hold values from 0 to 2
- tentative: bfloat16 [1024, 2, 256, 256], P(('gx', 'gy')), may hold values from -1.5 to 1.5
- inverse_diagonal: bfloat16 [1024, 256, 256], P(('gx', 'gy')), may hold values from -0.375 to 0.375
- peer_sends: int32 [128, 32], P(('gx', 'gy')), may hold values from 0 to 7
- slab_sends: int32 [128, 2], P(('gx', 'gy')), may hold values from 0 to 7
- coarse_slots: int32 [1024, 2, 2], P(('gx', 'gy')), may hold values from 0 to 63, as said below
Outputs:
- smoothed: bfloat16 [1024, 2, 256, 256], P(('gx', 'gy'))
- coarse_operator: bfloat16 [256, 256, 256], P(('gx', 'gy'))
The draws below stay inside these ranges and needn't reach their ends.
Inputs may be any that keep to these rules, and one draw needn't show every extreme that they name: `match_slots`: the value 2 stands for no matching block. `coarse_slots`: no two partial blocks of one device name the same coarse block; coarse block c of a slab belongs to the device of gy index c // 2.
All inputs are finite; a program needn't handle non-finite values.
Results may differ from the reference program's by a relative error of at most 0.012.
Values may be sent and summed in bfloat16 or wider, within the bound.
No kernel may reach another device: no remote copies, remote signals or barrier semaphores. Data moves between devices by JAX's collectives and lax.ppermute only.
A program may use at most 128 MiB of HBM per device.

```python
import jax
import jax.numpy as jnp
from jax import lax

B = 256
R = 8
KL = 2
KO = 4
K = 6
KP = 2
S = 1
H = 1
NB = 1024
NEXT = 42
CS = 2
NCOARSE = 256
N_GX = 4
N_GY = 32


def draw_coarse_slots(key, part):
    devices = N_GX * N_GY
    total = N_GY * CS
    per_device = R * KP * KP
    key_bias, key_hot, key_noise, key_order = jax.random.split(key, 4)
    bias = jax.random.randint(key_bias, (N_GX, N_GY), 0, 4)
    hot = jax.random.randint(key_hot, (N_GX,), 0, N_GY)
    bias = jnp.where(jnp.arange(N_GY)[None, :] == hot[:, None], 4, bias)
    slot_ids = jnp.arange(total, dtype=jnp.int32)
    owner = slot_ids // CS
    slab = jnp.arange(devices, dtype=jnp.int32) // N_GY
    weight = bias[slab][:, owner]
    weight = jnp.where(((slot_ids == 0) | (slot_ids == total - 1))[None, :], 5, weight)
    noise = jax.random.randint(key_noise, (devices, total), 0, 65536)
    scores = (weight * 65536 + noise) * total + slot_ids[None, :]
    _, picked = lax.top_k(scores, per_device)
    order_keys = jax.random.randint(key_order, (devices, per_device), 0, 65536) * per_device + jnp.arange(per_device, dtype=jnp.int32)[None, :]
    order = jnp.argsort(order_keys, axis=1, stable=True)
    shuffled = jnp.take_along_axis(picked, order, axis=1)
    return shuffled.astype(jnp.int32).reshape(NB, KP, KP)


def touch_ends(values, stream_key, smallest, largest):
    index_at = [jax.random.randint(jax.random.fold_in(stream_key, axis), (), 0, length) for axis, length in enumerate(values.shape)]
    longest = values.shape.index(max(values.shape))
    neighbour = index_at[:longest] + [(index_at[longest] + 1) % values.shape[longest]] + index_at[longest + 1:]
    return values.at[tuple(index_at)].set(smallest).at[tuple(neighbour)].set(largest)


def levels(own_key, extent, cuts, smallest, high):
    def one(axis_at, blocks):
        heights = jax.random.uniform(jax.random.fold_in(jax.random.fold_in(own_key, 6), axis_at), (blocks,), jnp.float32, smallest / len(cuts), high / len(cuts))
        return jnp.repeat(jnp.exp(heights), extent[axis_at] // blocks).reshape((-1,) + (1,) * (len(extent) - axis_at - 1))

    factor_of = one(*cuts[0])
    for cut in cuts[1:]:
        factor_of = factor_of * one(*cut)
    return factor_of


def gaussian(own_key, shape, scale, bound, cuts=(), kind=jnp.bfloat16):
    factor_of = levels(own_key, shape, cuts, -0.22, 0.18) if cuts else 1.0
    array = jax.random.normal(own_key, shape, jnp.float32) * scale * factor_of
    return jnp.minimum(jnp.maximum(array, -bound), bound).astype(kind)


def setup_inputs(seed: int = 0) -> dict:
    key_of = jax.random.split(jax.random.key(seed), 10)
    return {
        "operator_blocks": gaussian(key_of[0], (NB, K, B, B), (K * B) ** -0.5, 0.15625, ((0, 128),)),
        "local_columns": touch_ends(jax.random.randint(key_of[1], (NB, KL), 0, R), jax.random.fold_in(key_of[1], 1), 0, R - 1).astype(jnp.int32),
        "remote_columns": touch_ends(jax.random.randint(key_of[2], (NB, KO), R, NEXT), jax.random.fold_in(key_of[2], 1), R, NEXT - 1).astype(jnp.int32),
        "match_slots": touch_ends(jax.random.randint(key_of[3], (NB, K, KP), 0, KP + 1), jax.random.fold_in(key_of[3], 1), 0, KP).astype(jnp.int32),
        "tentative": gaussian(key_of[4], (NB, KP, B, B), 0.25, 1.5, ((0, 128),)),
        "inverse_diagonal": gaussian(key_of[5], (NB, B, B), B ** -0.5, 0.375, ((0, 128),)),
        "peer_sends": touch_ends(jax.random.randint(key_of[6], (N_GX * N_GY, N_GY * S), 0, R), jax.random.fold_in(key_of[6], 1), 0, R - 1).astype(jnp.int32),
        "slab_sends": touch_ends(jax.random.randint(key_of[7], (N_GX * N_GY, 2 * H), 0, R), jax.random.fold_in(key_of[7], 1), 0, R - 1).astype(jnp.int32),
        "coarse_slots": draw_coarse_slots(jax.random.fold_in(key_of[9], 71), 0),
    }


def select_blocks(picked, matches):
    selected = []
    for out_block in range(matches.shape[2]):
        chosen = jnp.zeros_like(picked[:, :, 0])
        for in_block in range(picked.shape[2]):
            matched = (matches[:, :, out_block] == in_block)[:, :, None, None]
            chosen = jnp.where(matched, picked[:, :, in_block], chosen)
        selected.append(chosen)
    return jnp.stack(selected, axis=2)


def table_map(peer_sends, slab_sends):
    devices = N_GX * N_GY
    device = jnp.arange(devices, dtype=jnp.int32)
    slab = device // N_GY
    member = device % N_GY
    own_rows = device[:, None] * R + jnp.arange(R, dtype=jnp.int32)[None, :]
    entry = jnp.arange(N_GY * S, dtype=jnp.int32)
    source = slab[:, None] * N_GY + entry[None, :] // S
    position = member[:, None] * S + entry[None, :] % S
    peer_rows = source * R + peer_sends[source, position]
    below = jnp.clip(device - N_GY, 0, devices - 1)
    above = jnp.clip(device + N_GY, 0, devices - 1)
    lower_rows = jnp.where((slab >= 1)[:, None], below[:, None] * R + slab_sends[below, :H], NB)
    upper_rows = jnp.where((slab < N_GX - 1)[:, None], above[:, None] * R + slab_sends[above, H:], NB)
    return jnp.concatenate([own_rows, peer_rows, lower_rows, upper_rows], axis=1).astype(jnp.int32)


def product_rows(padded, blocks, columns, matches):
    picked = padded[columns].astype(jnp.float32)
    chosen = select_blocks(picked, matches)
    return jnp.einsum('rkab,rknbc->rnac', blocks.astype(jnp.float32), chosen, precision=lax.Precision.HIGHEST)


def reference(operator_blocks, local_columns, remote_columns, match_slots, tentative, inverse_diagonal, peer_sends, slab_sends, coarse_slots):
    devices = N_GX * N_GY
    lookup = table_map(peer_sends, slab_sends)
    columns = jnp.concatenate([local_columns, remote_columns], axis=1).astype(jnp.int32)
    owner_device = (jnp.arange(NB, dtype=jnp.int32) // R)[:, None]
    global_columns = lookup[owner_device, columns].astype(jnp.int32)
    blocks_dev = operator_blocks.reshape(devices, R, K, B, B)
    columns_dev = global_columns.reshape(devices, R, K)
    matches_dev = match_slots.reshape(devices, R, K, KP)
    inverse_dev = inverse_diagonal.reshape(devices, R, B, B)
    fine_rows = tentative
    for smooth_pass in range(2):
        padded = jnp.concatenate([fine_rows, jnp.zeros((1, KP, B, B), fine_rows.dtype)], axis=0)

        def smooth_device(inputs):
            blocks, device_columns, matches, inverse, rows = inputs
            image = lax.optimization_barrier(product_rows(padded, blocks, device_columns, matches).astype(jnp.bfloat16))
            update = jnp.einsum('rab,rnbc->rnac', inverse.astype(jnp.float32), image.astype(jnp.float32), precision=lax.Precision.HIGHEST)
            return (rows.astype(jnp.float32) - update).astype(jnp.bfloat16)

        fine_rows = lax.map(smooth_device, (blocks_dev, columns_dev, matches_dev, inverse_dev, fine_rows.reshape(devices, R, KP, B, B))).reshape(NB, KP, B, B)
    padded = jnp.concatenate([fine_rows, jnp.zeros((1, KP, B, B), fine_rows.dtype)], axis=0)
    slots_dev = coarse_slots.reshape(devices, R * KP * KP)

    def accumulate(total, inputs):
        blocks, device_columns, matches, rows, slots, device = inputs
        image = lax.optimization_barrier(product_rows(padded, blocks, device_columns, matches).astype(jnp.bfloat16))
        partial_value = jnp.einsum('rnab,rmac->rnmbc', rows.astype(jnp.float32), image.astype(jnp.float32), precision=lax.Precision.HIGHEST)
        partial_value = lax.optimization_barrier(partial_value.astype(jnp.bfloat16)).astype(jnp.float32).reshape(R * KP * KP, B, B)
        targets = (device // N_GY) * (N_GY * CS) + slots
        return total.at[targets].add(partial_value), None

    start = jnp.zeros((NCOARSE, B, B), jnp.float32)
    total, _ = lax.scan(accumulate, start, (blocks_dev, columns_dev, matches_dev, fine_rows.reshape(devices, R, KP, B, B), slots_dev, jnp.arange(devices, dtype=jnp.int32)))
    return fine_rows, total.astype(jnp.bfloat16)
```

```python
import functools

import jax
import jax.numpy as jnp
from jax import lax
from jax.experimental import pallas as pl
from jax.experimental.pallas import tpu as pltpu
from jax.sharding import Mesh
from jax.sharding import PartitionSpec as P

AXES = ("gx", "x", "y", "c")
GY = ("x", "y", "c")


def shifted(value, axis, steps):
    count = lax.axis_size(axis)
    first, last = (max(0, -steps), min(count, count - steps))
    return lax.ppermute(value, axis, [(source, source + steps) for source in range(first, last)])


def send_rows(peer_ref, slab_ref, rows_ref, out_ref, up_ref, down_ref, sems):
    copies = []
    for q in range(out_ref.shape[0]):
        copies.append(pltpu.make_async_copy(rows_ref.at[peer_ref[q]], out_ref.at[q], sems.at[q]))
    copies.append(pltpu.make_async_copy(rows_ref.at[slab_ref[0]], up_ref.at[0], sems.at[len(copies)]))
    copies.append(pltpu.make_async_copy(rows_ref.at[slab_ref[1]], down_ref.at[0], sems.at[len(copies)]))
    for copy in copies:
        copy.start()
    for copy in copies:
        copy.wait()


def outgoing_shapes(peers, blocks, width):
    one = jax.ShapeDtypeStruct((1, blocks, width, width), jnp.bfloat16)
    return (jax.ShapeDtypeStruct((peers, blocks, width, width), jnp.bfloat16), one, one)


def pack_kernel(peer_ref, slab_ref, rows_ref, out_ref, up_ref, down_ref, sems):
    send_rows(peer_ref, slab_ref, rows_ref, out_ref, up_ref, down_ref, sems)


def pack(peer_list, slab_list, rows):
    count, blocks, width, _ = rows.shape
    peers = peer_list.shape[0]
    anywhere = pl.BlockSpec(memory_space=pl.ANY)
    return pl.pallas_call(
        pack_kernel,
        grid_spec=pltpu.PrefetchScalarGridSpec(
            num_scalar_prefetch=2,
            grid=(1,),
            in_specs=[pl.BlockSpec(rows.shape, lambda i, *refs: (0, 0, 0, 0))],
            out_specs=[anywhere] * 3,
            scratch_shapes=[pltpu.SemaphoreType.DMA((peers + 2,))],
        ),
        out_shape=outgoing_shapes(peers, blocks, width),
        name="pack_rows",
    )(peer_list, slab_list, rows)


def gather_operand(columns, matches, own_ref, peers, low_ref, high_ref, rhs, i, own_count, peer_count):
    width = own_ref.shape[-1]
    local = 2
    for k in range(rhs.shape[0] // width):
        column = columns[i * 6 + k]
        for n in range(2):
            match = matches[(i * 6 + k) * 2 + n]
            there = jnp.minimum(match, 1)
            place = (pl.ds(k * width, width), pl.ds(n * width, width))

            @pl.when(match > 1)
            def _():
                rhs[place] = jnp.zeros((width, width), rhs.dtype)

            if k < local:

                @pl.when(match < 2)
                def _():
                    rhs[place] = own_ref[column, there]
            else:
                peer_ref = peers[k - local]

                @pl.when((match < 2) & (column < own_count + peer_count))
                def _():
                    rhs[place] = peer_ref[0, there]

                @pl.when((match < 2) & (column == own_count + peer_count))
                def _():
                    rhs[place] = low_ref[0, there]

                @pl.when((match < 2) & (column > own_count + peer_count))
                def _():
                    rhs[place] = high_ref[0, there]


def row_image(a_ref, rhs):
    lhs = jnp.concatenate([a_ref[0, k] for k in range(a_ref.shape[1])], axis=1)
    return jnp.dot(lhs, rhs[...], preferred_element_type=jnp.float32).astype(jnp.bfloat16)


def smooth_kernel(
    columns, matches, peer_list, slab_list,
    a_ref, d_ref, own_ref, r0, r1, r2, r3, low_ref, high_ref,
    rows_out, out_ref, up_ref, down_ref,
    rhs, kept, sems,
):
    i = pl.program_id(0)
    width = own_ref.shape[-1]
    gather_operand(columns, matches, own_ref, (r0, r1, r2, r3), low_ref, high_ref, rhs, i, own_ref.shape[0], out_ref.shape[0])
    image = row_image(a_ref, rhs)
    update = jnp.dot(d_ref[0], image, preferred_element_type=jnp.float32)
    for n in range(2):
        new = own_ref[i, n].astype(jnp.float32) - update[:, n * width : (n + 1) * width]
        new = new.astype(jnp.bfloat16)
        rows_out[0, n] = new
        kept[i, n] = new

    @pl.when(i == pl.num_programs(0) - 1)
    def _():
        send_rows(peer_list, slab_list, kept, out_ref, up_ref, down_ref, sems)


def final_kernel(
    columns, matches, slots, core,
    a_ref, own_ref, r0, r1, r2, r3, low_ref, high_ref,
    keep_ref, swap_ref,
    rhs,
):
    i = pl.program_id(0)
    width = own_ref.shape[-1]

    @pl.when(i == 0)
    def _():
        keep_ref[...] = jnp.zeros_like(keep_ref)
        swap_ref[...] = jnp.zeros_like(swap_ref)

    gather_operand(columns, matches, own_ref, (r0, r1, r2, r3), low_ref, high_ref, rhs, i, own_ref.shape[0], 32)
    image = row_image(a_ref, rhs)
    mine = jnp.concatenate([own_ref[i, n] for n in range(2)], axis=1)
    partial = lax.dot_general(mine, image, (((0,), (0,)), ((), ())), preferred_element_type=jnp.float32)
    partial = partial.astype(jnp.bfloat16)
    for n1 in range(2):
        for n2 in range(2):
            slot = slots[(i * 2 + n1) * 2 + n2]
            owner = slot // 2
            place = (owner // 2) * 2 + slot % 2
            block = partial[n1 * width : (n1 + 1) * width, n2 * width : (n2 + 1) * width]

            @pl.when(owner % 2 == core[0])
            def _():
                keep_ref[place] = block

            @pl.when(owner % 2 != core[0])
            def _():
                swap_ref[place] = block


def operand_specs(rows, blocks, width, inner, peers):
    def peer_spec(k):
        def index(i, columns, *refs):
            return (jnp.clip(columns[i * inner + k] - rows, 0, peers - 1), 0, 0, 0)

        return pl.BlockSpec((1, blocks, width, width), index)

    whole = pl.BlockSpec((rows, blocks, width, width), lambda i, *refs: (0, 0, 0, 0))
    single = pl.BlockSpec((1, blocks, width, width), lambda i, *refs: (0, 0, 0, 0))
    return [whole, *[peer_spec(k) for k in range(2, inner)], single, single]


def smooth(tables, peer_list, slab_list, operator, inverse, rows, received, low, high):
    count, inner, width, _ = operator.shape
    blocks = rows.shape[1]
    peers = received.shape[0]
    anywhere = pl.BlockSpec(memory_space=pl.ANY)
    outs = outgoing_shapes(peers, blocks, width)
    return pl.pallas_call(
        smooth_kernel,
        grid_spec=pltpu.PrefetchScalarGridSpec(
            num_scalar_prefetch=4,
            grid=(count,),
            in_specs=[
                pl.BlockSpec((1, inner, width, width), lambda i, *refs: (i, 0, 0, 0)),
                pl.BlockSpec((1, width, width), lambda i, *refs: (i, 0, 0)),
                *operand_specs(count, blocks, width, inner, peers),
            ],
            out_specs=[pl.BlockSpec((1, blocks, width, width), lambda i, *refs: (i, 0, 0, 0)), anywhere, anywhere, anywhere],
            scratch_shapes=[
                pltpu.VMEM((inner * width, blocks * width), jnp.bfloat16),
                pltpu.VMEM((count, blocks, width, width), jnp.bfloat16),
                pltpu.SemaphoreType.DMA((peers + 2,)),
            ],
        ),
        out_shape=(jax.ShapeDtypeStruct(rows.shape, jnp.bfloat16), *outs),
        compiler_params=pltpu.CompilerParams(vmem_limit_bytes=40 << 20),
        name="smooth_rows",
    )(*tables, peer_list, slab_list, operator, inverse, rows, received, received, received, received, low, high)


def galerkin(tables, slots, core, operator, rows, received, low, high):
    count, inner, width, _ = operator.shape
    blocks = rows.shape[1]
    peers = received.shape[0]
    half = jax.ShapeDtypeStruct((peers, width, width), jnp.bfloat16)
    half_spec = pl.BlockSpec((peers, width, width), lambda i, *refs: (0, 0, 0))
    return pl.pallas_call(
        final_kernel,
        grid_spec=pltpu.PrefetchScalarGridSpec(
            num_scalar_prefetch=4,
            grid=(count,),
            in_specs=[
                pl.BlockSpec((1, inner, width, width), lambda i, *refs: (i, 0, 0, 0)),
                *operand_specs(count, blocks, width, inner, peers),
            ],
            out_specs=[half_spec, half_spec],
            scratch_shapes=[pltpu.VMEM((inner * width, blocks * width), jnp.bfloat16)],
        ),
        out_shape=(half, half),
        compiler_params=pltpu.CompilerParams(vmem_limit_bytes=48 << 20),
        name="galerkin_rows",
    )(*tables, slots, core, operator, rows, received, received, received, received, low, high)


def body(
    operator_blocks,
    local_columns,
    remote_columns,
    match_slots,
    tentative,
    inverse_diagonal,
    peer_sends,
    slab_sends,
    coarse_slots,
):
    peer_list = peer_sends.reshape(-1)
    slab_list = slab_sends.reshape(-1)
    columns = jnp.concatenate([local_columns, remote_columns], axis=1).reshape(-1)
    tables = (columns, match_slots.reshape(-1))
    core = lax.axis_index("c").reshape(1).astype(jnp.int32)

    def exchange(outgoing, up, down):
        received = lax.all_to_all(outgoing, GY, split_axis=0, concat_axis=0, tiled=True)
        return received, shifted(up, "gx", 1), shifted(down, "gx", -1)

    rows = tentative
    outgoing = pack(peer_list, slab_list, rows)
    for smooth_pass in range(2):
        arrived = exchange(*outgoing)
        rows, *outgoing = smooth(tables, peer_list, slab_list, operator_blocks, inverse_diagonal, rows, *arrived)
    arrived = exchange(*outgoing)
    keep, swap = galerkin(tables, coarse_slots.reshape(-1), core, operator_blocks, rows, *arrived)
    other = lax.ppermute(swap, "c", [(0, 1), (1, 0)])
    chip = (keep.astype(jnp.float32) + other.astype(jnp.float32)).astype(jnp.bfloat16)
    width = chip.shape[-1]
    received = lax.all_to_all(chip, ("x", "y"), split_axis=0, concat_axis=0, tiled=True)
    coarse = jnp.sum(received.reshape(-1, 2, width, width), axis=0, dtype=jnp.float32)
    return (rows, coarse.astype(jnp.bfloat16))


def solution(mesh):
    fine = Mesh(mesh.devices.reshape(4, 4, 4, 2), AXES)
    placed = tuple(P(AXES, *[None] * extra) for extra in (3, 1, 1, 2, 3, 2, 1, 1, 2))
    return jax.shard_map(
        body,
        mesh=fine,
        in_specs=placed,
        out_specs=(P(AXES, None, None, None), P(AXES, None, None)),
        check_vma=False,
    )
```

```python
import jax
import jax.numpy as jnp
from jax import lax
from jax.experimental import pallas as pl
from jax.experimental.pallas import tpu as pltpu
from jax.sharding import Mesh
from jax.sharding import PartitionSpec as P

AXES = ("gx", "x", "y", "c")
GY = ("x", "y", "c")
LINKS = 6
LOCAL = 2


def shifted(value, axis, steps):
    count = lax.axis_size(axis)
    first, last = (max(0, -steps), min(count, count - steps))
    return lax.ppermute(value, axis, [(source, source + steps) for source in range(first, last)])


def pack_kernel(peer_ref, rows_ref, out_ref, sems):
    copies = []
    for q in range(out_ref.shape[0]):
        copies.append(pltpu.make_async_copy(rows_ref.at[peer_ref[q]], out_ref.at[q], sems.at[q]))
    for copy in copies:
        copy.start()
    for copy in copies:
        copy.wait()


def pack(peer_list, rows):
    count, blocks, width, _ = rows.shape
    peers = peer_list.shape[0]
    size = 2 * blocks * width * width
    return pl.pallas_call(
        pack_kernel,
        grid_spec=pltpu.PrefetchScalarGridSpec(
            num_scalar_prefetch=1,
            grid=(1,),
            in_specs=[pl.BlockSpec(rows.shape, lambda i, *refs: (0, 0, 0, 0))],
            out_specs=pl.BlockSpec(memory_space=pl.ANY),
            scratch_shapes=[pltpu.SemaphoreType.DMA((peers,))],
        ),
        out_shape=jax.ShapeDtypeStruct((peers, blocks, width, width), jnp.bfloat16),
        cost_estimate=pl.CostEstimate(flops=0, transcendentals=0, bytes_accessed=(count + 2 * peers) * size),
        compiler_params=pltpu.CompilerParams(vmem_limit_bytes=56 << 20),
        name="pack_rows",
    )(peer_list, rows)


def fetch_rows(columns, i, slot, peers_ref, low_ref, high_ref, far, sems, first, count):
    for k in range(far.shape[1]):
        column = columns[i * LINKS + LOCAL + k]
        place = (far.at[slot, k], sems.at[slot, k])

        @pl.when(column < first + count)
        def _():
            pltpu.make_async_copy(peers_ref.at[jnp.maximum(column - first, 0)], *place).start()

        @pl.when(column == first + count)
        def _():
            pltpu.make_async_copy(low_ref.at[0], *place).start()

        @pl.when(column > first + count)
        def _():
            pltpu.make_async_copy(high_ref.at[0], *place).start()


def row_image(columns, matches, a_ref, own_ref, peers_ref, low_ref, high_ref, rhs, lhs, far, sems):
    i = pl.program_id(0)
    slot = lax.rem(i, 2)
    width = own_ref.shape[-1]
    arrays = (peers_ref, low_ref, high_ref, far, sems, own_ref.shape[0], peers_ref.shape[0])

    @pl.when(i == 0)
    def _():
        fetch_rows(columns, i, slot, *arrays)

    @pl.when(i + 1 < pl.num_programs(0))
    def _():
        fetch_rows(columns, i + 1, 1 - slot, *arrays)

    for k in range(far.shape[1]):
        pltpu.make_async_copy(peers_ref.at[0], far.at[slot, k], sems.at[slot, k]).wait()
    for k in range(LINKS):
        lhs[:, k * width : (k + 1) * width] = a_ref[0, k]
        for n in range(2):
            match = matches[(i * LINKS + k) * 2 + n]
            there = jnp.minimum(match, 1)
            if k < LOCAL:
                block = own_ref[columns[i * LINKS + k], there]
            else:
                block = far[slot, k - LOCAL, there]
            block = jnp.where(match < 2, block, jnp.zeros_like(block))
            rhs[k * width : (k + 1) * width, n * width : (n + 1) * width] = block
    return jnp.dot(lhs[...], rhs[...], preferred_element_type=jnp.float32).astype(jnp.bfloat16)


def smooth_kernel(
    columns, matches, slab_list,
    a_ref, d_ref, own_ref, peers_ref, low_ref, high_ref,
    rows_out, up_ref, down_ref,
    rhs, lhs, far, kept, sems, out_sems,
):
    i = pl.program_id(0)
    width = own_ref.shape[-1]
    image = row_image(columns, matches, a_ref, own_ref, peers_ref, low_ref, high_ref, rhs, lhs, far, sems)
    update = jnp.dot(d_ref[0], image, preferred_element_type=jnp.float32)
    for n in range(2):
        new = own_ref[i, n].astype(jnp.float32) - update[:, n * width : (n + 1) * width]
        new = new.astype(jnp.bfloat16)
        rows_out[0, n] = new
        kept[i, n] = new

    @pl.when(i == pl.num_programs(0) - 1)
    def _():
        up = pltpu.make_async_copy(kept.at[slab_list[0]], up_ref.at[0], out_sems.at[0])
        down = pltpu.make_async_copy(kept.at[slab_list[1]], down_ref.at[0], out_sems.at[1])
        up.start()
        down.start()
        up.wait()
        down.wait()


def final_kernel(
    columns, matches, slots, core,
    a_ref, own_ref, peers_ref, low_ref, high_ref,
    keep_ref, swap_ref,
    rhs, lhs, far, sems,
):
    i = pl.program_id(0)
    width = own_ref.shape[-1]

    @pl.when(i == 0)
    def _():
        keep_ref[...] = jnp.zeros_like(keep_ref)
        swap_ref[...] = jnp.zeros_like(swap_ref)

    image = row_image(columns, matches, a_ref, own_ref, peers_ref, low_ref, high_ref, rhs, lhs, far, sems)
    mine = jnp.concatenate([own_ref[i, n] for n in range(2)], axis=1)
    partial = lax.dot_general(mine, image, (((0,), (0,)), ((), ())), preferred_element_type=jnp.float32)
    partial = partial.astype(jnp.bfloat16)
    for n1 in range(2):
        for n2 in range(2):
            slot = slots[(i * 2 + n1) * 2 + n2]
            owner = slot // 2
            place = (owner // 2) * 2 + slot % 2
            block = partial[n1 * width : (n1 + 1) * width, n2 * width : (n2 + 1) * width]

            @pl.when(owner % 2 == core[0])
            def _():
                keep_ref[place] = block

            @pl.when(owner % 2 != core[0])
            def _():
                swap_ref[place] = block


def gather_scratch(blocks, width):
    return [
        pltpu.VMEM((LINKS * width, blocks * width), jnp.bfloat16),
        pltpu.VMEM((width, LINKS * width), jnp.bfloat16),
        pltpu.VMEM((2, LINKS - LOCAL, blocks, width, width), jnp.bfloat16),
    ]


def smooth(tables, slab_list, operator, inverse, rows, received, low, high):
    count, inner, width, _ = operator.shape
    blocks = rows.shape[1]
    anywhere = pl.BlockSpec(memory_space=pl.ANY)
    one = jax.ShapeDtypeStruct((1, blocks, width, width), jnp.bfloat16)
    return pl.pallas_call(
        smooth_kernel,
        grid_spec=pltpu.PrefetchScalarGridSpec(
            num_scalar_prefetch=3,
            grid=(count,),
            in_specs=[
                pl.BlockSpec((1, inner, width, width), lambda i, *refs: (i, 0, 0, 0)),
                pl.BlockSpec((1, width, width), lambda i, *refs: (i, 0, 0)),
                pl.BlockSpec(rows.shape, lambda i, *refs: (0, 0, 0, 0)),
                anywhere,
                anywhere,
                anywhere,
            ],
            out_specs=[pl.BlockSpec((1, blocks, width, width), lambda i, *refs: (i, 0, 0, 0)), anywhere, anywhere],
            scratch_shapes=[
                *gather_scratch(blocks, width),
                pltpu.VMEM((count, blocks, width, width), jnp.bfloat16),
                pltpu.SemaphoreType.DMA((2, LINKS - LOCAL)),
                pltpu.SemaphoreType.DMA((2,)),
            ],
        ),
        out_shape=(jax.ShapeDtypeStruct(rows.shape, jnp.bfloat16), one, one),
        compiler_params=pltpu.CompilerParams(vmem_limit_bytes=56 << 20),
        name="smooth_rows",
    )(*tables, slab_list, operator, inverse, rows, received, low, high)


def galerkin(tables, slots, core, operator, rows, received, low, high):
    count, inner, width, _ = operator.shape
    blocks = rows.shape[1]
    peers = received.shape[0]
    anywhere = pl.BlockSpec(memory_space=pl.ANY)
    half = jax.ShapeDtypeStruct((peers, width, width), jnp.bfloat16)
    half_spec = pl.BlockSpec((peers, width, width), lambda i, *refs: (0, 0, 0))
    return pl.pallas_call(
        final_kernel,
        grid_spec=pltpu.PrefetchScalarGridSpec(
            num_scalar_prefetch=4,
            grid=(count,),
            in_specs=[
                pl.BlockSpec((1, inner, width, width), lambda i, *refs: (i, 0, 0, 0)),
                pl.BlockSpec(rows.shape, lambda i, *refs: (0, 0, 0, 0)),
                anywhere,
                anywhere,
                anywhere,
            ],
            out_specs=[half_spec, half_spec],
            scratch_shapes=[*gather_scratch(blocks, width), pltpu.SemaphoreType.DMA((2, LINKS - LOCAL))],
        ),
        out_shape=(half, half),
        compiler_params=pltpu.CompilerParams(vmem_limit_bytes=56 << 20),
        name="galerkin_rows",
    )(*tables, slots, core, operator, rows, received, low, high)


def body(
    operator_blocks,
    local_columns,
    remote_columns,
    match_slots,
    tentative,
    inverse_diagonal,
    peer_sends,
    slab_sends,
    coarse_slots,
):
    peer_list = peer_sends.reshape(-1)
    slab_list = slab_sends.reshape(-1)
    columns = jnp.concatenate([local_columns, remote_columns], axis=1).reshape(-1)
    tables = (columns, match_slots.reshape(-1))
    core = lax.axis_index("c").reshape(1).astype(jnp.int32)

    slots = coarse_slots.reshape(-1)

    def exchange(rows, up, down):
        low, high = shifted(up, "gx", 1), shifted(down, "gx", -1)
        outgoing = pack(peer_list, rows)
        outgoing, low, high, *now = lax.optimization_barrier((outgoing, low, high, *tables, slab_list, slots, core, rows))
        received = lax.all_to_all(outgoing, GY, split_axis=0, concat_axis=0, tiled=True)
        return now, received, low, high

    up, down = tentative[slab_list[:1]], tentative[slab_list[1:]]
    rows = tentative
    for smooth_pass in range(2):
        (*tables, slab_list, slots, core, rows), *arrived = exchange(rows, up, down)
        rows, up, down = smooth(tables, slab_list, operator_blocks, inverse_diagonal, rows, *arrived)
    (*tables, slab_list, slots, core, rows), *arrived = exchange(rows, up, down)
    keep, swap = galerkin(tables, slots, core, operator_blocks, rows, *arrived)
    other = lax.ppermute(swap, "c", [(0, 1), (1, 0)])
    chip = (keep.astype(jnp.float32) + other.astype(jnp.float32)).astype(jnp.bfloat16)
    width = chip.shape[-1]
    received = lax.all_to_all(chip, ("x", "y"), split_axis=0, concat_axis=0, tiled=True)
    coarse = jnp.sum(received.reshape(-1, 2, width, width), axis=0, dtype=jnp.float32)
    return (rows, coarse.astype(jnp.bfloat16))


def solution(mesh):
    fine = Mesh(mesh.devices.reshape(4, 4, 4, 2), AXES)
    placed = tuple(P(AXES, *[None] * extra) for extra in (3, 1, 1, 2, 3, 2, 1, 1, 2))
    return jax.shard_map(
        body,
        mesh=fine,
        in_specs=placed,
        out_specs=(P(AXES, None, None, None), P(AXES, None, None)),
        check_vma=False,
    )
```

```python
import jax
import jax.numpy as jnp
from jax import lax
from jax.experimental import pallas as pl
from jax.experimental.pallas import tpu as pltpu
from jax.sharding import Mesh
from jax.sharding import PartitionSpec as P

AXES = ("gx", "x", "y", "c")
GY = ("x", "y", "c")
LINKS = 6
LOCAL = 2
BLOCKS = 2
RING = 4
ANY = pl.BlockSpec(memory_space=pl.ANY)
SMEM = pl.BlockSpec(memory_space=pltpu.SMEM)
PARAMS = pltpu.CompilerParams(vmem_limit_bytes=56 << 20)


def shifted(value, axis, steps):
    count = lax.axis_size(axis)
    first, last = (max(0, -steps), min(count, count - steps))
    return lax.ppermute(value, axis, [(source, source + steps) for source in range(first, last)])


def around(value, axis, steps):
    count = lax.axis_size(axis)
    return lax.ppermute(value, axis, [(source, (source + steps) % count) for source in range(count)])


def shape(*sizes):
    return jax.ShapeDtypeStruct(sizes, jnp.bfloat16)


def pick_kernel(slab, rows_ref, up_ref, down_ref, held, sems):
    arrivals = [pltpu.make_async_copy(rows_ref.at[slab[0, j]], held.at[j], sems.at[j]) for j in range(2)]
    copies = [pltpu.make_async_copy(held.at[j], out.at[0], sems.at[2 + j]) for j, out in enumerate((up_ref, down_ref))]
    for copy in arrivals:
        copy.start()
    for arrival, copy in zip(arrivals, copies):
        arrival.wait()
        copy.start()
    for copy in copies:
        copy.wait()


def pick(slab, rows):
    one = shape(1, *rows.shape[1:])
    return pl.pallas_call(
        pick_kernel,
        in_specs=[SMEM, ANY],
        out_specs=[ANY, ANY],
        out_shape=(one, one),
        scratch_shapes=[pltpu.VMEM((2, *rows.shape[1:]), jnp.bfloat16), pltpu.SemaphoreType.DMA((4,))],
        compiler_params=PARAMS,
        name="pick_rows",
    )(slab, rows)


def pack_kernel(peer, rows_ref, out_ref, own, in_sems, sems):
    arrivals = [pltpu.make_async_copy(rows_ref.at[j], own.at[j], in_sems.at[j]) for j in range(own.shape[0])]
    for copy in arrivals:
        copy.start()
    for copy in arrivals:
        copy.wait()
    copies = [pltpu.make_async_copy(own.at[peer[0, q]], out_ref.at[q], sems.at[q]) for q in range(out_ref.shape[0])]
    for copy in copies:
        copy.start()
    for copy in copies:
        copy.wait()


def pack(peer, rows):
    peers = peer.shape[1]
    return pl.pallas_call(
        pack_kernel,
        in_specs=[SMEM, ANY],
        out_specs=ANY,
        out_shape=shape(peers, *rows.shape[1:]),
        scratch_shapes=[
            pltpu.VMEM(rows.shape, jnp.bfloat16),
            pltpu.SemaphoreType.DMA((rows.shape[0],)),
            pltpu.SemaphoreType.DMA((peers,)),
        ],
        cost_estimate=pl.CostEstimate(flops=0, transcendentals=0, bytes_accessed=10 << 20),
        compiler_params=PARAMS,
        name="pack_rows",
    )(peer, rows)


def start_row(remote, i, a_hbm, peers_hbm, low_hbm, high_hbm, a_buf, far, sems, first, count):
    pltpu.make_async_copy(a_hbm.at[i], a_buf.at[i], sems.at[i, 0]).start()
    for k in range(LINKS - LOCAL):
        column = remote[k, i]
        place = (far.at[i, k], sems.at[i, 1 + k])

        @pl.when(column < first + count)
        def _():
            pltpu.make_async_copy(peers_hbm.at[jnp.maximum(column - first, 0)], *place).start()

        @pl.when(column == first + count)
        def _():
            pltpu.make_async_copy(low_hbm.at[0], *place).start()

        @pl.when(column > first + count)
        def _():
            pltpu.make_async_copy(high_hbm.at[0], *place).start()


def wait_row(i, a_hbm, peers_hbm, a_buf, far, sems):
    pltpu.make_async_copy(a_hbm.at[i], a_buf.at[i], sems.at[i, 0]).wait()
    for k in range(LINKS - LOCAL):
        pltpu.make_async_copy(peers_hbm.at[0], far.at[i, k], sems.at[i, 1 + k]).wait()


def row_image(local, match, i, a_buf, own, far, rhs):
    width = own.shape[-1]
    for k in range(LINKS):
        for n in range(BLOCKS):
            wanted = match[k, n, i]
            there = jnp.minimum(wanted, BLOCKS - 1)
            if k < LOCAL:
                block = own[local[k, i], there]
            else:
                block = far[i, k - LOCAL, there]
            block = jnp.where(wanted < BLOCKS, block, jnp.zeros_like(block))
            rhs[k * width : (k + 1) * width, n * width : (n + 1) * width] = block
    lhs = jnp.concatenate([a_buf[i, k] for k in range(LINKS)], axis=1)
    return jnp.dot(lhs, rhs[...], preferred_element_type=jnp.float32).astype(jnp.bfloat16)


def smooth_kernel(
    local, remote, match, peer, slab,
    a_hbm, d_hbm, own_hbm, peers_hbm, low_hbm, high_hbm,
    rows_hbm, out_hbm, up_hbm, down_hbm,
    a_buf, d_buf, own, far, new, rhs,
    sems, own_sems, d_sem, rows_sem, out_sem, slab_sems,
):
    count, width = own.shape[0], own.shape[-1]
    peers = out_hbm.shape[0]
    arrays = (a_hbm, peers_hbm, low_hbm, high_hbm, a_buf, far, sems, count, peers)
    own_copy = pltpu.make_async_copy(own_hbm, own, own_sems.at[0])
    d_copy = pltpu.make_async_copy(d_hbm, d_buf, d_sem.at[0])
    own_copy.start()
    start_row(remote, 0, *arrays)
    d_copy.start()

    @pl.loop(1, count)
    def _(i):
        start_row(remote, i, *arrays)

    own_copy.wait()

    @pl.loop(0, count)
    def _(i):
        wait_row(i, a_hbm, peers_hbm, a_buf, far, sems)
        image = row_image(local, match, i, a_buf, own, far, rhs)

        @pl.when(i == 0)
        def _():
            d_copy.wait()

        update = jnp.dot(d_buf[i], image, preferred_element_type=jnp.float32)
        for n in range(BLOCKS):
            value = own[i, n].astype(jnp.float32) - update[:, n * width : (n + 1) * width]
            new[i, n] = value.astype(jnp.bfloat16)
        pltpu.make_async_copy(new.at[i], rows_hbm.at[i], rows_sem.at[0]).start()
        for q in range(peers):

            @pl.when(peer[0, q] == i)
            def _():
                pltpu.make_async_copy(new.at[i], out_hbm.at[q], out_sem.at[0]).start()

    up = pltpu.make_async_copy(new.at[slab[0, 0]], up_hbm.at[0], slab_sems.at[0])
    down = pltpu.make_async_copy(new.at[slab[0, 1]], down_hbm.at[0], slab_sems.at[1])
    up.start()
    down.start()
    pltpu.make_async_copy(rows_hbm, rows_hbm, rows_sem.at[0]).wait()
    pltpu.make_async_copy(out_hbm, out_hbm, out_sem.at[0]).wait()
    up.wait()
    down.wait()


def row_scratch(count, width):
    return [
        pltpu.VMEM((count, LINKS, width, width), jnp.bfloat16),
        pltpu.VMEM((count, BLOCKS, width, width), jnp.bfloat16),
        pltpu.VMEM((count, LINKS - LOCAL, BLOCKS, width, width), jnp.bfloat16),
        pltpu.VMEM((LINKS * width, BLOCKS * width), jnp.bfloat16),
        pltpu.SemaphoreType.DMA((count, 1 + LINKS - LOCAL)),
        pltpu.SemaphoreType.DMA((1,)),
    ]


def smooth(tables, peer, slab, operator, inverse, rows, received, low, high):
    count, _, width, _ = operator.shape
    one = shape(1, *rows.shape[1:])
    a_buf, own, far, rhs, sems, single = row_scratch(count, width)
    return pl.pallas_call(
        smooth_kernel,
        in_specs=[SMEM] * 5 + [ANY] * 6,
        out_specs=[ANY] * 4,
        out_shape=(shape(*rows.shape), shape(*received.shape), one, one),
        scratch_shapes=[
            a_buf, pltpu.VMEM(inverse.shape, jnp.bfloat16), own, far, own, rhs,
            sems, single, single, single, single, pltpu.SemaphoreType.DMA((2,)),
        ],
        compiler_params=PARAMS,
        name="smooth_rows",
    )(*tables, peer, slab, operator, inverse, rows, received, low, high)


def galerkin_kernel(
    local, remote, match, slots, here,
    a_hbm, own_hbm, peers_hbm, low_hbm, high_hbm,
    keep_hbm, swap_hbm,
    a_buf, own, far, rhs, result, zero, named,
    sems, own_sems, keep_sem, swap_sem,
):
    count, width = own.shape[0], own.shape[-1]
    peers = peers_hbm.shape[0]
    half = keep_hbm.shape[0]
    arrays = (a_hbm, peers_hbm, low_hbm, high_hbm, a_buf, far, sems, count, peers)
    own_copy = pltpu.make_async_copy(own_hbm, own, own_sems.at[0])
    own_copy.start()

    @pl.loop(0, count)
    def _(i):
        start_row(remote, i, *arrays)

    zero[...] = jnp.zeros_like(zero)

    def send(block, slot):
        owner = slot // 2
        chip = owner // 2
        dx = (chip // RING - here[0] + RING) % RING
        dy = (chip % RING - here[1] + RING) % RING
        second = slot % 2
        place = jnp.where(second == 0, dx * RING + dy, RING * RING + dy * RING + dx)

        @pl.when(owner % 2 == here[2])
        def _():
            pltpu.make_async_copy(block, keep_hbm.at[place], keep_sem.at[0]).start()

        @pl.when(owner % 2 != here[2])
        def _():
            pltpu.make_async_copy(block, swap_hbm.at[place], swap_sem.at[0]).start()

    @pl.loop(0, 2 * half)
    def _(slot):
        named[slot] = 0

    @pl.loop(0, count)
    def _(i):
        for n1 in range(BLOCKS):
            for n2 in range(BLOCKS):
                named[slots[n1, n2, i]] = 1

    @pl.loop(0, 2 * half)
    def _(slot):
        @pl.when(named[slot] == 0)
        def _():
            send(zero, slot)

    own_copy.wait()

    @pl.loop(0, count)
    def _(i):
        wait_row(i, a_hbm, peers_hbm, a_buf, far, sems)
        image = row_image(local, match, i, a_buf, own, far, rhs)
        mine = jnp.concatenate([own[i, n] for n in range(BLOCKS)], axis=1)
        partial = lax.dot_general(mine, image, (((0,), (0,)), ((), ())), preferred_element_type=jnp.float32)
        for n1 in range(BLOCKS):
            for n2 in range(BLOCKS):
                block = partial[n1 * width : (n1 + 1) * width, n2 * width : (n2 + 1) * width]
                result[i, n1 * BLOCKS + n2] = block.astype(jnp.bfloat16)
                send(result.at[i, n1 * BLOCKS + n2], slots[n1, n2, i])

    pltpu.make_async_copy(keep_hbm, keep_hbm, keep_sem.at[0]).wait()
    pltpu.make_async_copy(swap_hbm, swap_hbm, swap_sem.at[0]).wait()


def galerkin(tables, slots, here, operator, rows, received, low, high):
    count, _, width, _ = operator.shape
    half = RING * RING * BLOCKS
    a_buf, own, far, rhs, sems, single = row_scratch(count, width)
    return pl.pallas_call(
        galerkin_kernel,
        in_specs=[SMEM] * 5 + [ANY] * 5,
        out_specs=[ANY] * 2,
        out_shape=(shape(half, width, width), shape(half, width, width)),
        scratch_shapes=[
            a_buf, own, far, rhs,
            pltpu.VMEM((count, BLOCKS * BLOCKS, width, width), jnp.bfloat16),
            pltpu.VMEM((width, width), jnp.bfloat16),
            pltpu.SMEM((2 * half,), jnp.int32),
            sems, single, single, single,
        ],
        compiler_params=PARAMS,
        name="galerkin_rows",
    )(*tables, slots, here, operator, rows, received, low, high)


def add(terms):
    total = terms[0].astype(jnp.float32)
    for term in terms[1:]:
        total = total + term.astype(jnp.float32)
    return total.astype(jnp.bfloat16)


def body(
    operator_blocks,
    local_columns,
    remote_columns,
    match_slots,
    tentative,
    inverse_diagonal,
    peer,
    slab,
    coarse_slots,
):
    tables = (local_columns.T, remote_columns.T, match_slots.transpose(1, 2, 0))
    slots = coarse_slots.transpose(1, 2, 0)
    here = jnp.stack([lax.axis_index("x"), lax.axis_index("y"), lax.axis_index("c")]).astype(jnp.int32)
    rows = tentative
    up, down = pick(slab, rows)
    low, high = shifted(up, "gx", 1), shifted(down, "gx", -1)
    outgoing = pack(peer, rows)
    outgoing, low, high, here = lax.optimization_barrier((outgoing, low, high, here))
    received = lax.all_to_all(outgoing, GY, split_axis=0, concat_axis=0, tiled=True)
    for smooth_pass in range(2):
        rows, outgoing, up, down = smooth(tables, peer, slab, operator_blocks, inverse_diagonal, rows, received, low, high)
        low, high = shifted(up, "gx", 1), shifted(down, "gx", -1)
        outgoing, low, high = lax.optimization_barrier((outgoing, low, high))
        received = lax.all_to_all(outgoing, GY, split_axis=0, concat_axis=0, tiled=True)
    keep, swap = galerkin(tables, slots, here, operator_blocks, rows, received, low, high)
    other = lax.ppermute(swap, "c", [(0, 1), (1, 0)])
    parts = [add((keep[RING * j : RING * j + RING], other[RING * j : RING * j + RING])) for j in range(2 * RING)]
    for axes in (("x", "y"), ("y", "x")):
        sums = []
        for axis, group in zip(axes, (parts[: len(parts) // 2], parts[len(parts) // 2 :])):
            terms = [group[0], *[around(group[s], axis, s) for s in range(1, RING)]]
            sums.append([add([term[j : j + 1] for term in terms]) for j in range(terms[0].shape[0])])
        parts = sums[0] + sums[1]
    return (rows, jnp.concatenate(parts, axis=0))


def solution(mesh):
    fine = Mesh(mesh.devices.reshape(4, 4, 4, 2), AXES)
    placed = tuple(P(AXES, *[None] * extra) for extra in (3, 1, 1, 2, 3, 2, 1, 1, 2))
    return jax.shard_map(
        body,
        mesh=fine,
        in_specs=placed,
        out_specs=(P(AXES, None, None, None), P(AXES, None, None)),
        check_vma=False,
    )
```

```python
import jax
import jax.numpy as jnp
from jax import lax
from jax.experimental import pallas as pl
from jax.experimental.pallas import tpu as pltpu
from jax.sharding import Mesh
from jax.sharding import PartitionSpec as P

AXES = ("gx", "x", "y", "c")
GY = ("x", "y", "c")
LINKS = 6
LOCAL = 2
BLOCKS = 2
RING = 4
ANY = pl.BlockSpec(memory_space=pl.ANY)
VMEM = pl.BlockSpec(memory_space=pltpu.VMEM)
SMEM = pl.BlockSpec(memory_space=pltpu.SMEM)
PARAMS = pltpu.CompilerParams(vmem_limit_bytes=40 << 20)


def shifted(value, axis, steps):
    count = lax.axis_size(axis)
    first, last = (max(0, -steps), min(count, count - steps))
    return lax.ppermute(value, axis, [(source, source + steps) for source in range(first, last)])


def around(value, steps, swapped):
    pairs = []
    for x in range(RING):
        for y in range(RING):
            for c in range(2):
                to_x, to_y = ((x + steps) % RING, y) if c == swapped else (x, (y + steps) % RING)
                pairs.append(((x * RING + y) * 2 + c, (to_x * RING + to_y) * 2 + c))
    return lax.ppermute(value, GY, pairs)


def shape(*sizes):
    return jax.ShapeDtypeStruct(sizes, jnp.bfloat16)


def pick_kernel(slab, rows_ref, up_ref, down_ref, held, sems):
    arrivals = [pltpu.make_async_copy(rows_ref.at[slab[0, j]], held.at[j], sems.at[j]) for j in range(2)]
    copies = [pltpu.make_async_copy(held.at[j], out.at[0], sems.at[2 + j]) for j, out in enumerate((up_ref, down_ref))]
    for copy in arrivals:
        copy.start()
    for arrival, copy in zip(arrivals, copies):
        arrival.wait()
        copy.start()
    for copy in copies:
        copy.wait()


def pick(slab, rows):
    one = shape(1, *rows.shape[1:])
    return pl.pallas_call(
        pick_kernel,
        in_specs=[SMEM, ANY],
        out_specs=[ANY, ANY],
        out_shape=(one, one),
        scratch_shapes=[pltpu.VMEM((2, *rows.shape[1:]), jnp.bfloat16), pltpu.SemaphoreType.DMA((4,))],
        compiler_params=PARAMS,
        name="pick_rows",
    )(slab, rows)


def pack_kernel(peer, rows_ref, out_ref, own, in_sems, sems):
    arrivals = [pltpu.make_async_copy(rows_ref.at[j], own.at[j], in_sems.at[j]) for j in range(own.shape[0])]
    for copy in arrivals:
        copy.start()
    for copy in arrivals:
        copy.wait()
    copies = [pltpu.make_async_copy(own.at[peer[0, q]], out_ref.at[q], sems.at[q]) for q in range(out_ref.shape[0])]
    for copy in copies:
        copy.start()
    for copy in copies:
        copy.wait()


def pack(peer, rows):
    peers = peer.shape[1]
    return pl.pallas_call(
        pack_kernel,
        in_specs=[SMEM, ANY],
        out_specs=ANY,
        out_shape=shape(peers, *rows.shape[1:]),
        scratch_shapes=[
            pltpu.VMEM(rows.shape, jnp.bfloat16),
            pltpu.SemaphoreType.DMA((rows.shape[0],)),
            pltpu.SemaphoreType.DMA((peers,)),
        ],
        cost_estimate=pl.CostEstimate(flops=0, transcendentals=0, bytes_accessed=10 << 20),
        compiler_params=PARAMS,
        name="pack_rows",
    )(peer, rows)


def start_row(remote, i, peers_hbm, low_hbm, high_hbm, far, sems, first, count):
    for k in range(LINKS - LOCAL):
        column = remote[k, i]
        place = (far.at[i, k], sems.at[i, k])

        @pl.when(column < first + count)
        def _():
            pltpu.make_async_copy(peers_hbm.at[jnp.maximum(column - first, 0)], *place).start()

        @pl.when(column == first + count)
        def _():
            pltpu.make_async_copy(low_hbm.at[0], *place).start()

        @pl.when(column > first + count)
        def _():
            pltpu.make_async_copy(high_hbm.at[0], *place).start()


def wait_row(i, peers_hbm, far, sems):
    for k in range(LINKS - LOCAL):
        pltpu.make_async_copy(peers_hbm.at[0], far.at[i, k], sems.at[i, k]).wait()


def row_image(local, match, i, a_buf, own, far, rhs):
    width = own.shape[-1]
    for k in range(LINKS):
        for n in range(BLOCKS):
            wanted = match[k, n, i]
            there = jnp.minimum(wanted, BLOCKS - 1)
            if k < LOCAL:
                block = own[local[k, i], there]
            else:
                block = far[i, k - LOCAL, there]
            block = jnp.where(wanted < BLOCKS, block, jnp.zeros_like(block))
            rhs[k * width : (k + 1) * width, n * width : (n + 1) * width] = block
    lhs = jnp.concatenate([a_buf[i, k] for k in range(LINKS)], axis=1)
    return jnp.dot(lhs, rhs[...], preferred_element_type=jnp.float32).astype(jnp.bfloat16)


def smooth_kernel(
    local, remote, match, peer, slab,
    a_buf, d_buf, own, peers_hbm, low_hbm, high_hbm,
    rows_hbm, out_hbm, up_hbm, down_hbm,
    far, new, rhs,
    sems, rows_sem, out_sem, slab_sems,
):
    count, width = own.shape[0], own.shape[-1]
    peers = out_hbm.shape[0]
    arrays = (peers_hbm, low_hbm, high_hbm, far, sems, count, peers)

    @pl.loop(0, count)
    def _(i):
        start_row(remote, i, *arrays)

    @pl.loop(0, count)
    def _(i):
        wait_row(i, peers_hbm, far, sems)
        image = row_image(local, match, i, a_buf, own, far, rhs)

        update = jnp.dot(d_buf[i], image, preferred_element_type=jnp.float32)
        for n in range(BLOCKS):
            value = own[i, n].astype(jnp.float32) - update[:, n * width : (n + 1) * width]
            new[i, n] = value.astype(jnp.bfloat16)
        pltpu.make_async_copy(new.at[i], rows_hbm.at[i], rows_sem.at[0]).start()
        for q in range(peers):

            @pl.when(peer[0, q] == i)
            def _():
                pltpu.make_async_copy(new.at[i], out_hbm.at[q], out_sem.at[0]).start()

    up = pltpu.make_async_copy(new.at[slab[0, 0]], up_hbm.at[0], slab_sems.at[0])
    down = pltpu.make_async_copy(new.at[slab[0, 1]], down_hbm.at[0], slab_sems.at[1])
    up.start()
    down.start()
    pltpu.make_async_copy(rows_hbm, rows_hbm, rows_sem.at[0]).wait()
    pltpu.make_async_copy(out_hbm, out_hbm, out_sem.at[0]).wait()
    up.wait()
    down.wait()


def row_scratch(count, width):
    return [
        pltpu.VMEM((count, LINKS - LOCAL, BLOCKS, width, width), jnp.bfloat16),
        pltpu.VMEM((LINKS * width, BLOCKS * width), jnp.bfloat16),
        pltpu.SemaphoreType.DMA((count, LINKS - LOCAL)),
        pltpu.SemaphoreType.DMA((1,)),
    ]


def smooth(tables, peer, slab, operator, inverse, rows, received, low, high):
    count, _, width, _ = operator.shape
    one = shape(1, *rows.shape[1:])
    far, rhs, sems, single = row_scratch(count, width)
    return pl.pallas_call(
        smooth_kernel,
        in_specs=[SMEM] * 5 + [VMEM] * 3 + [ANY] * 3,
        out_specs=[ANY] * 4,
        out_shape=(shape(*rows.shape), shape(*received.shape), one, one),
        scratch_shapes=[
            far, pltpu.VMEM(rows.shape, jnp.bfloat16), rhs,
            sems, single, single, pltpu.SemaphoreType.DMA((2,)),
        ],
        compiler_params=PARAMS,
        name="smooth_rows",
    )(*tables, peer, slab, operator, inverse, rows, received, low, high)


def galerkin_kernel(
    local, remote, match, slots, here,
    a_buf, own, peers_hbm, low_hbm, high_hbm,
    keep_hbm, swap_hbm,
    far, rhs, result, zero, named,
    sems, keep_sem, swap_sem,
):
    count, width = own.shape[0], own.shape[-1]
    peers = peers_hbm.shape[0]
    half = keep_hbm.shape[0]
    arrays = (peers_hbm, low_hbm, high_hbm, far, sems, count, peers)

    @pl.loop(0, count)
    def _(i):
        start_row(remote, i, *arrays)

    zero[...] = jnp.zeros_like(zero)

    def send(block, slot):
        owner = slot // 2
        chip = owner // 2
        dx = (chip // RING - here[0] + RING) % RING
        dy = (chip % RING - here[1] + RING) % RING
        second = slot % 2
        place = jnp.where(second == 0, dx * RING + dy, dy * RING + dx) * 2 + owner % 2

        @pl.when(second == here[2])
        def _():
            pltpu.make_async_copy(block, keep_hbm.at[place], keep_sem.at[0]).start()

        @pl.when(second != here[2])
        def _():
            pltpu.make_async_copy(block, swap_hbm.at[place], swap_sem.at[0]).start()

    @pl.loop(0, 2 * half)
    def _(slot):
        named[slot] = 0

    @pl.loop(0, count)
    def _(i):
        for n1 in range(BLOCKS):
            for n2 in range(BLOCKS):
                named[slots[n1, n2, i]] = 1

    @pl.loop(0, 2 * half)
    def _(slot):
        @pl.when(named[slot] == 0)
        def _():
            send(zero, slot)

    @pl.loop(0, count)
    def _(i):
        wait_row(i, peers_hbm, far, sems)
        image = row_image(local, match, i, a_buf, own, far, rhs)
        mine = jnp.concatenate([own[i, n] for n in range(BLOCKS)], axis=1)
        partial = lax.dot_general(mine, image, (((0,), (0,)), ((), ())), preferred_element_type=jnp.float32)
        for n1 in range(BLOCKS):
            for n2 in range(BLOCKS):
                block = partial[n1 * width : (n1 + 1) * width, n2 * width : (n2 + 1) * width]
                result[i, n1 * BLOCKS + n2] = block.astype(jnp.bfloat16)
                send(result.at[i, n1 * BLOCKS + n2], slots[n1, n2, i])

    pltpu.make_async_copy(keep_hbm, keep_hbm, keep_sem.at[0]).wait()
    pltpu.make_async_copy(swap_hbm, swap_hbm, swap_sem.at[0]).wait()


def galerkin(tables, slots, here, operator, rows, received, low, high):
    count, _, width, _ = operator.shape
    half = RING * RING * BLOCKS
    far, rhs, sems, single = row_scratch(count, width)
    return pl.pallas_call(
        galerkin_kernel,
        in_specs=[SMEM] * 5 + [VMEM] * 2 + [ANY] * 3,
        out_specs=[ANY] * 2,
        out_shape=(shape(half, width, width), shape(half, width, width)),
        scratch_shapes=[
            far, rhs,
            pltpu.VMEM((count, BLOCKS * BLOCKS, width, width), jnp.bfloat16),
            pltpu.VMEM((width, width), jnp.bfloat16),
            pltpu.SMEM((2 * half,), jnp.int32),
            sems, single, single,
        ],
        compiler_params=PARAMS,
        name="galerkin_rows",
    )(*tables, slots, here, operator, rows, received, low, high)


def add(terms):
    total = terms[0].astype(jnp.float32)
    for term in terms[1:]:
        total = total + term.astype(jnp.float32)
    return total.astype(jnp.bfloat16)


def body(
    operator_blocks,
    local_columns,
    remote_columns,
    match_slots,
    tentative,
    inverse_diagonal,
    peer,
    slab,
    coarse_slots,
):
    tables = (local_columns.T, remote_columns.T, match_slots.transpose(1, 2, 0))
    slots = coarse_slots.transpose(1, 2, 0)
    here = jnp.stack([lax.axis_index("x"), lax.axis_index("y"), lax.axis_index("c")]).astype(jnp.int32)
    rows = tentative
    up, down = pick(slab, rows)
    low, high = shifted(up, "gx", 1), shifted(down, "gx", -1)
    outgoing = pack(peer, rows)
    outgoing, low, high, here = lax.optimization_barrier((outgoing, low, high, here))
    received = lax.all_to_all(outgoing, GY, split_axis=0, concat_axis=0, tiled=True)
    for smooth_pass in range(2):
        rows, outgoing, up, down = smooth(tables, peer, slab, operator_blocks, inverse_diagonal, rows, received, low, high)
        low, high = shifted(up, "gx", 1), shifted(down, "gx", -1)
        outgoing, low, high = lax.optimization_barrier((outgoing, low, high))
        received = lax.all_to_all(outgoing, GY, split_axis=0, concat_axis=0, tiled=True)
    keep, swap = galerkin(tables, slots, here, operator_blocks, rows, received, low, high)
    other = lax.ppermute(swap, "c", [(0, 1), (1, 0)])
    group = keep.shape[0] // RING
    parts = [add((keep[group * j : group * j + group], other[group * j : group * j + group])) for j in range(RING)]
    for swapped in range(2):
        terms = [parts[0], *[around(parts[s], s, swapped) for s in range(1, RING)]]
        group = max(terms[0].shape[0] // RING, 2)
        parts = [add([term[j : j + group] for term in terms]) for j in range(0, terms[0].shape[0], group)]
    total = parts[0]
    core = lax.axis_index("c") == 0
    mine = jnp.where(core, total[:1], total[1:])
    theirs = lax.ppermute(jnp.where(core, total[1:], total[:1]), "c", [(0, 1), (1, 0)])
    first, second = jnp.where(core, mine, theirs), jnp.where(core, theirs, mine)
    return (rows, jnp.concatenate([first, second], axis=0))


def solution(mesh):
    fine = Mesh(mesh.devices.reshape(4, 4, 4, 2), AXES)
    placed = tuple(P(AXES, *[None] * extra) for extra in (3, 1, 1, 2, 3, 2, 1, 1, 2))
    return jax.shard_map(
        body,
        mesh=fine,
        in_specs=placed,
        out_specs=(P(AXES, None, None, None), P(AXES, None, None)),
        check_vma=False,
    )
```

```python
import jax
import jax.numpy as jnp
from jax import lax
from jax.experimental import pallas as pl
from jax.experimental.pallas import tpu as pltpu
from jax.sharding import Mesh
from jax.sharding import PartitionSpec as P

AXES = ("gx", "x", "y", "c")
GY = ("x", "y", "c")
LINKS = 6
LOCAL = 2
BLOCKS = 2
RING = 4
ANY = pl.BlockSpec(memory_space=pl.ANY)
VMEM = pl.BlockSpec(memory_space=pltpu.VMEM)
SMEM = pl.BlockSpec(memory_space=pltpu.SMEM)
PARAMS = pltpu.CompilerParams(vmem_limit_bytes=40 << 20)


def shifted(value, axis, steps):
    count = lax.axis_size(axis)
    first, last = (max(0, -steps), min(count, count - steps))
    return lax.ppermute(value, axis, [(source, source + steps) for source in range(first, last)])


def around(value, steps, swapped):
    pairs = []
    for x in range(RING):
        for y in range(RING):
            for c in range(2):
                to_x, to_y = ((x + steps) % RING, y) if c == swapped else (x, (y + steps) % RING)
                pairs.append(((x * RING + y) * 2 + c, (to_x * RING + to_y) * 2 + c))
    return lax.ppermute(value, GY, pairs)


def shape(*sizes):
    return jax.ShapeDtypeStruct(sizes, jnp.bfloat16)


def pick_kernel(slab, rows_ref, up_ref, down_ref, held, sems):
    arrivals = [pltpu.make_async_copy(rows_ref.at[slab[0, j]], held.at[j], sems.at[j]) for j in range(2)]
    copies = [pltpu.make_async_copy(held.at[j], out.at[0], sems.at[2 + j]) for j, out in enumerate((up_ref, down_ref))]
    for copy in arrivals:
        copy.start()
    for arrival, copy in zip(arrivals, copies):
        arrival.wait()
        copy.start()
    for copy in copies:
        copy.wait()


def pick(slab, rows):
    one = shape(1, *rows.shape[1:])
    return pl.pallas_call(
        pick_kernel,
        in_specs=[SMEM, ANY],
        out_specs=[ANY, ANY],
        out_shape=(one, one),
        scratch_shapes=[pltpu.VMEM((2, *rows.shape[1:]), jnp.bfloat16), pltpu.SemaphoreType.DMA((4,))],
        compiler_params=PARAMS,
        name="pick_rows",
    )(slab, rows)


def pack_kernel(peer, rows_ref, out_ref, own, in_sems, sems):
    arrivals = [pltpu.make_async_copy(rows_ref.at[j], own.at[j], in_sems.at[j]) for j in range(own.shape[0])]
    for copy in arrivals:
        copy.start()
    for copy in arrivals:
        copy.wait()
    copies = [pltpu.make_async_copy(own.at[peer[0, q]], out_ref.at[q], sems.at[q]) for q in range(out_ref.shape[0])]
    for copy in copies:
        copy.start()
    for copy in copies:
        copy.wait()


def pack(peer, rows):
    peers = peer.shape[1]
    return pl.pallas_call(
        pack_kernel,
        in_specs=[SMEM, ANY],
        out_specs=ANY,
        out_shape=shape(peers, *rows.shape[1:]),
        scratch_shapes=[
            pltpu.VMEM(rows.shape, jnp.bfloat16),
            pltpu.SemaphoreType.DMA((rows.shape[0],)),
            pltpu.SemaphoreType.DMA((peers,)),
        ],
        cost_estimate=pl.CostEstimate(flops=0, transcendentals=0, bytes_accessed=10 << 20),
        compiler_params=PARAMS,
        name="pack_rows",
    )(peer, rows)


def start_row(remote, i, slot, peers_hbm, low_hbm, high_hbm, far, sems, first, count):
    for k in range(LINKS - LOCAL):
        column = remote[k, i]
        place = (far.at[slot, k], sems.at[slot, k])

        @pl.when(column < first + count)
        def _():
            pltpu.make_async_copy(peers_hbm.at[jnp.maximum(column - first, 0)], *place).start()

        @pl.when(column == first + count)
        def _():
            pltpu.make_async_copy(low_hbm.at[0], *place).start()

        @pl.when(column > first + count)
        def _():
            pltpu.make_async_copy(high_hbm.at[0], *place).start()


def wait_row(i, peers_hbm, far, sems):
    for k in range(LINKS - LOCAL):
        pltpu.make_async_copy(peers_hbm.at[0], far.at[i, k], sems.at[i, k]).wait()


def row_image(local, match, i, slot, a_buf, own, far, rhs):
    width = own.shape[-1]
    for k in range(LINKS):
        for n in range(BLOCKS):
            wanted = match[k, n, i]
            there = jnp.minimum(wanted, BLOCKS - 1)
            if k < LOCAL:
                block = own[local[k, i], there]
            else:
                block = far[slot, k - LOCAL, there]
            block = jnp.where(wanted < BLOCKS, block, jnp.zeros_like(block))
            rhs[k * width : (k + 1) * width, n * width : (n + 1) * width] = block
    lhs = jnp.concatenate([a_buf[i, k] for k in range(LINKS)], axis=1)
    return jnp.dot(lhs, rhs[...], preferred_element_type=jnp.float32).astype(jnp.bfloat16)


def new_row(local, match, i, slot, a_buf, d_buf, own, far, rhs):
    width = own.shape[-1]
    image = row_image(local, match, i, slot, a_buf, own, far, rhs)
    update = jnp.dot(d_buf[i], image, preferred_element_type=jnp.float32)
    halves = [update[:, n * width : (n + 1) * width] for n in range(BLOCKS)]
    return [(own[i, n].astype(jnp.float32) - halves[n]).astype(jnp.bfloat16) for n in range(BLOCKS)]


def slab_kernel(
    local, remote, match, slab,
    a_buf, d_buf, own, peers_hbm, low_hbm, high_hbm,
    up, down,
    far, rhs,
    sems,
):
    arrays = (peers_hbm, low_hbm, high_hbm, far, sems, own.shape[0], peers_hbm.shape[0])
    for j in range(2):
        start_row(remote, slab[0, j], j, *arrays)
    for j, out in enumerate((up, down)):
        wait_row(j, peers_hbm, far, sems)
        for n, value in enumerate(new_row(local, match, slab[0, j], j, a_buf, d_buf, own, far, rhs)):
            out[0, n] = value


def smooth_kernel(
    local, remote, match, peer,
    a_buf, d_buf, own, peers_hbm, low_hbm, high_hbm,
    rows_hbm, out_hbm,
    far, new, rhs,
    sems, rows_sem, out_sem,
):
    count = own.shape[0]
    peers = out_hbm.shape[0]
    arrays = (peers_hbm, low_hbm, high_hbm, far, sems, count, peers)

    @pl.loop(0, count)
    def _(i):
        start_row(remote, i, i, *arrays)

    @pl.loop(0, count)
    def _(i):
        wait_row(i, peers_hbm, far, sems)
        for n, value in enumerate(new_row(local, match, i, i, a_buf, d_buf, own, far, rhs)):
            new[i, n] = value
        pltpu.make_async_copy(new.at[i], rows_hbm.at[i], rows_sem.at[0]).start()
        for q in range(peers):

            @pl.when(peer[0, q] == i)
            def _():
                pltpu.make_async_copy(new.at[i], out_hbm.at[q], out_sem.at[0]).start()

    pltpu.make_async_copy(rows_hbm, rows_hbm, rows_sem.at[0]).wait()
    pltpu.make_async_copy(out_hbm, out_hbm, out_sem.at[0]).wait()


def row_scratch(count, width):
    return [
        pltpu.VMEM((count, LINKS - LOCAL, BLOCKS, width, width), jnp.bfloat16),
        pltpu.VMEM((LINKS * width, BLOCKS * width), jnp.bfloat16),
        pltpu.SemaphoreType.DMA((count, LINKS - LOCAL)),
        pltpu.SemaphoreType.DMA((1,)),
    ]


def slab_rows(tables, slab, operator, inverse, rows, received, low, high):
    width = operator.shape[-1]
    one = shape(1, *rows.shape[1:])
    return pl.pallas_call(
        slab_kernel,
        in_specs=[SMEM] * 4 + [VMEM] * 3 + [ANY] * 3,
        out_specs=[VMEM] * 2,
        out_shape=(one, one),
        scratch_shapes=row_scratch(2, width)[:3],
        compiler_params=PARAMS,
        name="slab_rows",
    )(*tables, slab, operator, inverse, rows, received, low, high)


def smooth(tables, peer, operator, inverse, rows, received, low, high):
    count, _, width, _ = operator.shape
    far, rhs, sems, single = row_scratch(count, width)
    flops = 2 * count * (LINKS + 1) * BLOCKS * width**3
    return pl.pallas_call(
        smooth_kernel,
        in_specs=[SMEM] * 4 + [VMEM] * 3 + [ANY] * 3,
        out_specs=[ANY] * 2,
        out_shape=(shape(*rows.shape), shape(*received.shape)),
        scratch_shapes=[far, pltpu.VMEM(rows.shape, jnp.bfloat16), rhs, sems, single, single],
        cost_estimate=pl.CostEstimate(flops=flops, transcendentals=0, bytes_accessed=28 << 20),
        compiler_params=PARAMS,
        name="smooth_rows",
    )(*tables, peer, operator, inverse, rows, received, low, high)


def galerkin_kernel(
    local, remote, match, slots, here,
    a_buf, own, peers_hbm, low_hbm, high_hbm,
    keep, swap,
    far, rhs,
    sems,
):
    count, width = own.shape[0], own.shape[-1]
    peers = peers_hbm.shape[0]
    arrays = (peers_hbm, low_hbm, high_hbm, far, sems, count, peers)

    @pl.loop(0, count)
    def _(i):
        start_row(remote, i, i, *arrays)

    keep[...] = jnp.zeros_like(keep)
    swap[...] = jnp.zeros_like(swap)

    @pl.loop(0, count)
    def _(i):
        wait_row(i, peers_hbm, far, sems)
        image = row_image(local, match, i, i, a_buf, own, far, rhs)
        mine = jnp.concatenate([own[i, n] for n in range(BLOCKS)], axis=1)
        partial = lax.dot_general(mine, image, (((0,), (0,)), ((), ())), preferred_element_type=jnp.float32)
        for n1 in range(BLOCKS):
            for n2 in range(BLOCKS):
                block = partial[n1 * width : (n1 + 1) * width, n2 * width : (n2 + 1) * width]
                block = block.astype(jnp.bfloat16)
                slot = slots[n1, n2, i]
                owner = slot // 2
                chip = owner // 2
                dx = (chip // RING - here[0] + RING) % RING
                dy = (chip % RING - here[1] + RING) % RING
                second = slot % 2
                place = jnp.where(second == 0, dx * RING + dy, dy * RING + dx) * 2 + owner % 2

                @pl.when(second == here[2])
                def _():
                    keep[place] = block

                @pl.when(second != here[2])
                def _():
                    swap[place] = block


def galerkin(tables, slots, here, operator, rows, received, low, high):
    count, _, width, _ = operator.shape
    half = RING * RING * BLOCKS
    far, rhs, sems, single = row_scratch(count, width)
    return pl.pallas_call(
        galerkin_kernel,
        in_specs=[SMEM] * 5 + [VMEM] * 2 + [ANY] * 3,
        out_specs=[VMEM] * 2,
        out_shape=(shape(half, width, width), shape(half, width, width)),
        scratch_shapes=[far, rhs, sems],
        compiler_params=pltpu.CompilerParams(vmem_limit_bytes=30 << 20),
        name="galerkin_rows",
    )(*tables, slots, here, operator, rows, received, low, high)


def add(terms):
    total = terms[0].astype(jnp.float32)
    for term in terms[1:]:
        total = total + term.astype(jnp.float32)
    return total.astype(jnp.bfloat16)


def body(
    operator_blocks,
    local_columns,
    remote_columns,
    match_slots,
    tentative,
    inverse_diagonal,
    peer,
    slab,
    coarse_slots,
):
    tables = (local_columns.T, remote_columns.T, match_slots.transpose(1, 2, 0))
    slots = coarse_slots.transpose(1, 2, 0)
    here = jnp.stack([lax.axis_index("x"), lax.axis_index("y"), lax.axis_index("c")]).astype(jnp.int32)
    rows = tentative
    up, down = pick(slab, rows)
    low, high = shifted(up, "gx", 1), shifted(down, "gx", -1)
    outgoing = pack(peer, rows)
    outgoing, low, high, here = lax.optimization_barrier((outgoing, low, high, here))
    received = lax.all_to_all(outgoing, GY, split_axis=0, concat_axis=0, tiled=True)
    for smooth_pass in range(2):
        operands = (operator_blocks, inverse_diagonal, rows, received, low, high)
        up, down = slab_rows(tables, slab, *operands)
        up, down, operands = lax.optimization_barrier((up, down, operands))
        low, high = shifted(up, "gx", 1), shifted(down, "gx", -1)
        rows, outgoing = smooth(tables, peer, *operands)
        outgoing, low, high = lax.optimization_barrier((outgoing, low, high))
        received = lax.all_to_all(outgoing, GY, split_axis=0, concat_axis=0, tiled=True)
    keep, swap = galerkin(tables, slots, here, operator_blocks, rows, received, low, high)
    other = lax.ppermute(swap, "c", [(0, 1), (1, 0)])
    group = keep.shape[0] // RING
    parts = [add((keep[group * j : group * j + group], other[group * j : group * j + group])) for j in range(RING)]
    for swapped in range(2):
        terms = [parts[0], *[around(parts[s], s, swapped) for s in range(1, RING)]]
        group = max(terms[0].shape[0] // RING, 2)
        parts = [add([term[j : j + group] for term in terms]) for j in range(0, terms[0].shape[0], group)]
    total = parts[0]
    core = lax.axis_index("c") == 0
    mine = jnp.where(core, total[:1], total[1:])
    theirs = lax.ppermute(jnp.where(core, total[1:], total[:1]), "c", [(0, 1), (1, 0)])
    first, second = jnp.where(core, mine, theirs), jnp.where(core, theirs, mine)
    return (rows, jnp.concatenate([first, second], axis=0))


def solution(mesh):
    fine = Mesh(mesh.devices.reshape(4, 4, 4, 2), AXES)
    placed = tuple(P(AXES, *[None] * extra) for extra in (3, 1, 1, 2, 3, 2, 1, 1, 2))
    return jax.shard_map(
        body,
        mesh=fine,
        in_specs=placed,
        out_specs=(P(AXES, None, None, None), P(AXES, None, None)),
        check_vma=False,
    )
```

```python
import jax
import jax.numpy as jnp
from jax import lax
from jax.experimental import pallas as pl
from jax.experimental.pallas import tpu as pltpu
from jax.sharding import Mesh
from jax.sharding import PartitionSpec as P

AXES = ("gx", "x", "y", "c")
GY = ("x", "y", "c")
LINKS = 6
LOCAL = 2
BLOCKS = 2
RING = 4
ANY = pl.BlockSpec(memory_space=pl.ANY)
VMEM = pl.BlockSpec(memory_space=pltpu.VMEM)
SMEM = pl.BlockSpec(memory_space=pltpu.SMEM)
PARAMS = pltpu.CompilerParams(vmem_limit_bytes=40 << 20)


def shifted(value, axis, steps):
    count = lax.axis_size(axis)
    first, last = (max(0, -steps), min(count, count - steps))
    return lax.ppermute(value, axis, [(source, source + steps) for source in range(first, last)])


def around(value, steps, swapped):
    pairs = []
    for x in range(RING):
        for y in range(RING):
            for c in range(2):
                to_x, to_y = ((x + steps) % RING, y) if c == swapped else (x, (y + steps) % RING)
                pairs.append(((x * RING + y) * 2 + c, (to_x * RING + to_y) * 2 + c))
    return lax.ppermute(value, GY, pairs)


def shape(*sizes):
    return jax.ShapeDtypeStruct(sizes, jnp.bfloat16)


def pick_kernel(slab, rows_ref, up_ref, down_ref, held, sems):
    arrivals = [pltpu.make_async_copy(rows_ref.at[slab[0, j]], held.at[j], sems.at[j]) for j in range(2)]
    copies = [pltpu.make_async_copy(held.at[j], out.at[0], sems.at[2 + j]) for j, out in enumerate((up_ref, down_ref))]
    for copy in arrivals:
        copy.start()
    for arrival, copy in zip(arrivals, copies):
        arrival.wait()
        copy.start()
    for copy in copies:
        copy.wait()


def pick(slab, rows):
    one = shape(1, *rows.shape[1:])
    return pl.pallas_call(
        pick_kernel,
        in_specs=[SMEM, ANY],
        out_specs=[ANY, ANY],
        out_shape=(one, one),
        scratch_shapes=[pltpu.VMEM((2, *rows.shape[1:]), jnp.bfloat16), pltpu.SemaphoreType.DMA((4,))],
        compiler_params=PARAMS,
        name="pick_rows",
    )(slab, rows)


def pack_kernel(peer, rows_ref, out_ref, own, in_sems, sems):
    arrivals = [pltpu.make_async_copy(rows_ref.at[j], own.at[j], in_sems.at[j]) for j in range(own.shape[0])]
    for copy in arrivals:
        copy.start()
    for copy in arrivals:
        copy.wait()
    copies = [pltpu.make_async_copy(own.at[peer[0, q]], out_ref.at[q], sems.at[q]) for q in range(out_ref.shape[0])]
    for copy in copies:
        copy.start()
    for copy in copies:
        copy.wait()


def pack(peer, rows):
    peers = peer.shape[1]
    return pl.pallas_call(
        pack_kernel,
        in_specs=[SMEM, ANY],
        out_specs=ANY,
        out_shape=shape(peers, *rows.shape[1:]),
        scratch_shapes=[
            pltpu.VMEM(rows.shape, jnp.bfloat16),
            pltpu.SemaphoreType.DMA((rows.shape[0],)),
            pltpu.SemaphoreType.DMA((peers,)),
        ],
        cost_estimate=pl.CostEstimate(flops=0, transcendentals=0, bytes_accessed=10 << 20),
        compiler_params=PARAMS,
        name="pack_rows",
    )(peer, rows)


def wanted_blocks(match, i, k):
    for m in range(BLOCKS):
        needed = match[LOCAL + k, 0, i] == m
        for n in range(1, BLOCKS):
            needed = needed | (match[LOCAL + k, n, i] == m)
        yield m, needed


def start_row(remote, match, i, slot, peers_hbm, low_hbm, high_hbm, far, sems, first, count):
    for k in range(LINKS - LOCAL):
        column = remote[k, i]
        for m, needed in wanted_blocks(match, i, k):
            place = (far.at[slot, k, m], sems.at[slot, k, m])

            @pl.when(needed & (column < first + count))
            def _():
                pltpu.make_async_copy(peers_hbm.at[jnp.maximum(column - first, 0), m], *place).start()

            @pl.when(needed & (column == first + count))
            def _():
                pltpu.make_async_copy(low_hbm.at[0, m], *place).start()

            @pl.when(needed & (column > first + count))
            def _():
                pltpu.make_async_copy(high_hbm.at[0, m], *place).start()


def wait_row(match, i, slot, peers_hbm, far, sems):
    for k in range(LINKS - LOCAL):
        for m, needed in wanted_blocks(match, i, k):

            @pl.when(needed)
            def _():
                pltpu.make_async_copy(peers_hbm.at[0, m], far.at[slot, k, m], sems.at[slot, k, m]).wait()


def row_image(local, match, i, slot, a_buf, own, far, rhs):
    width = own.shape[-1]
    for k in range(LINKS):
        for n in range(BLOCKS):
            wanted = match[k, n, i]
            there = jnp.minimum(wanted, BLOCKS - 1)
            if k < LOCAL:
                block = own[local[k, i], there]
            else:
                block = far[slot, k - LOCAL, there]
            block = jnp.where(wanted < BLOCKS, block, jnp.zeros_like(block))
            rhs[k * width : (k + 1) * width, n * width : (n + 1) * width] = block
    lhs = jnp.concatenate([a_buf[i, k] for k in range(LINKS)], axis=1)
    return jnp.dot(lhs, rhs[...], preferred_element_type=jnp.float32).astype(jnp.bfloat16)


def new_row(local, match, i, slot, a_buf, d_buf, own, far, rhs):
    width = own.shape[-1]
    image = row_image(local, match, i, slot, a_buf, own, far, rhs)
    update = jnp.dot(d_buf[i], image, preferred_element_type=jnp.float32)
    halves = [update[:, n * width : (n + 1) * width] for n in range(BLOCKS)]
    return [(own[i, n].astype(jnp.float32) - halves[n]).astype(jnp.bfloat16) for n in range(BLOCKS)]


def slab_kernel(
    local, remote, match, slab,
    a_buf, d_buf, own, peers_hbm, low_hbm, high_hbm,
    up, down,
    far, rhs,
    sems,
):
    arrays = (peers_hbm, low_hbm, high_hbm, far, sems, own.shape[0], peers_hbm.shape[0])
    for j in range(2):
        start_row(remote, match, slab[0, j], j, *arrays)
    for j, out in enumerate((up, down)):
        wait_row(match, slab[0, j], j, peers_hbm, far, sems)
        for n, value in enumerate(new_row(local, match, slab[0, j], j, a_buf, d_buf, own, far, rhs)):
            out[0, n] = value


def smooth_kernel(
    local, remote, match, peer,
    a_buf, d_buf, own, peers_hbm, low_hbm, high_hbm,
    rows_hbm, out_hbm,
    far, new, rhs,
    sems, rows_sem, out_sem,
):
    count = own.shape[0]
    peers = out_hbm.shape[0]
    arrays = (peers_hbm, low_hbm, high_hbm, far, sems, count, peers)

    @pl.loop(0, count)
    def _(i):
        start_row(remote, match, i, i, *arrays)

    @pl.loop(0, count)
    def _(i):
        wait_row(match, i, i, peers_hbm, far, sems)
        for n, value in enumerate(new_row(local, match, i, i, a_buf, d_buf, own, far, rhs)):
            new[i, n] = value
        pltpu.make_async_copy(new.at[i], rows_hbm.at[i], rows_sem.at[0]).start()
        for q in range(peers):

            @pl.when(peer[0, q] == i)
            def _():
                pltpu.make_async_copy(new.at[i], out_hbm.at[q], out_sem.at[0]).start()

    pltpu.make_async_copy(rows_hbm, rows_hbm, rows_sem.at[0]).wait()
    pltpu.make_async_copy(out_hbm, out_hbm, out_sem.at[0]).wait()


def row_scratch(count, width):
    return [
        pltpu.VMEM((count, LINKS - LOCAL, BLOCKS, width, width), jnp.bfloat16),
        pltpu.VMEM((LINKS * width, BLOCKS * width), jnp.bfloat16),
        pltpu.SemaphoreType.DMA((count, LINKS - LOCAL, BLOCKS)),
        pltpu.SemaphoreType.DMA((1,)),
    ]


def slab_rows(tables, slab, operator, inverse, rows, received, low, high):
    width = operator.shape[-1]
    one = shape(1, *rows.shape[1:])
    return pl.pallas_call(
        slab_kernel,
        in_specs=[SMEM] * 4 + [VMEM] * 3 + [ANY] * 3,
        out_specs=[VMEM] * 2,
        out_shape=(one, one),
        scratch_shapes=row_scratch(2, width)[:3],
        compiler_params=PARAMS,
        name="slab_rows",
    )(*tables, slab, operator, inverse, rows, received, low, high)


def smooth(tables, peer, operator, inverse, rows, received, low, high):
    count, _, width, _ = operator.shape
    far, rhs, sems, single = row_scratch(count, width)
    flops = 2 * count * (LINKS + 1) * BLOCKS * width**3
    return pl.pallas_call(
        smooth_kernel,
        in_specs=[SMEM] * 4 + [VMEM] * 3 + [ANY] * 3,
        out_specs=[ANY] * 2,
        out_shape=(shape(*rows.shape), shape(*received.shape)),
        scratch_shapes=[far, pltpu.VMEM(rows.shape, jnp.bfloat16), rhs, sems, single, single],
        cost_estimate=pl.CostEstimate(flops=flops, transcendentals=0, bytes_accessed=28 << 20),
        compiler_params=PARAMS,
        name="smooth_rows",
    )(*tables, peer, operator, inverse, rows, received, low, high)


def galerkin_kernel(
    local, remote, match, slots, here,
    a_buf, own, peers_hbm, low_hbm, high_hbm,
    *refs,
):
    keeps, swaps = refs[:RING], refs[RING : 2 * RING]
    far, rhs, sems = refs[2 * RING :]
    count, width = own.shape[0], own.shape[-1]
    peers = peers_hbm.shape[0]
    arrays = (peers_hbm, low_hbm, high_hbm, far, sems, count, peers)

    @pl.loop(0, count)
    def _(i):
        start_row(remote, match, i, i, *arrays)

    for out in keeps + swaps:
        out[...] = jnp.zeros_like(out)

    @pl.loop(0, count)
    def _(i):
        wait_row(match, i, i, peers_hbm, far, sems)
        image = row_image(local, match, i, i, a_buf, own, far, rhs)
        mine = jnp.concatenate([own[i, n] for n in range(BLOCKS)], axis=1)
        partial = lax.dot_general(mine, image, (((0,), (0,)), ((), ())), preferred_element_type=jnp.float32)
        for n1 in range(BLOCKS):
            for n2 in range(BLOCKS):
                block = partial[n1 * width : (n1 + 1) * width, n2 * width : (n2 + 1) * width]
                block = block.astype(jnp.bfloat16)
                slot = slots[n1, n2, i]
                owner = slot // 2
                chip = owner // 2
                dx = (chip // RING - here[0] + RING) % RING
                dy = (chip % RING - here[1] + RING) % RING
                second = slot % 2
                step = jnp.where(second == 0, dx, dy)
                place = jnp.where(second == 0, dy, dx) * 2 + owner % 2
                for j in range(RING):

                    @pl.when((second == here[2]) & (step == j))
                    def _():
                        keeps[j][place] = block

                    @pl.when((second != here[2]) & (step == j))
                    def _():
                        swaps[j][place] = block


def galerkin(tables, slots, here, operator, rows, received, low, high):
    count, _, width, _ = operator.shape
    far, rhs, sems, single = row_scratch(count, width)
    return pl.pallas_call(
        galerkin_kernel,
        in_specs=[SMEM] * 5 + [VMEM] * 2 + [ANY] * 3,
        out_specs=[VMEM] * (2 * RING),
        out_shape=[shape(2 * RING, width, width)] * (2 * RING),
        scratch_shapes=[far, rhs, sems],
        compiler_params=pltpu.CompilerParams(vmem_limit_bytes=30 << 20),
        name="galerkin_rows",
    )(*tables, slots, here, operator, rows, received, low, high)


def add(terms):
    total = terms[0].astype(jnp.float32)
    for term in terms[1:]:
        total = total + term.astype(jnp.float32)
    return total.astype(jnp.bfloat16)


def body(
    operator_blocks,
    local_columns,
    remote_columns,
    match_slots,
    tentative,
    inverse_diagonal,
    peer,
    slab,
    coarse_slots,
):
    tables = (local_columns.T, remote_columns.T, match_slots.transpose(1, 2, 0))
    slots = coarse_slots.transpose(1, 2, 0)
    here = jnp.stack([lax.axis_index("x"), lax.axis_index("y"), lax.axis_index("c")]).astype(jnp.int32)
    rows = tentative
    up, down = pick(slab, rows)
    low, high = shifted(up, "gx", 1), shifted(down, "gx", -1)
    outgoing = pack(peer, rows)
    outgoing, low, high, here = lax.optimization_barrier((outgoing, low, high, here))
    received = lax.all_to_all(outgoing, GY, split_axis=0, concat_axis=0, tiled=True)
    for smooth_pass in range(2):
        operands = (operator_blocks, inverse_diagonal, rows, received, low, high)
        up, down = slab_rows(tables, slab, *operands)
        up, down, operands = lax.optimization_barrier((up, down, operands))
        low, high = shifted(up, "gx", 1), shifted(down, "gx", -1)
        rows, outgoing = smooth(tables, peer, *operands)
        outgoing, low, high = lax.optimization_barrier((outgoing, low, high))
        received = lax.all_to_all(outgoing, GY, split_axis=0, concat_axis=0, tiled=True)
    parts = galerkin(tables, slots, here, operator_blocks, rows, received, low, high)
    keeps, swaps = parts[:RING], parts[RING:]
    others = [lax.ppermute(swap, "c", [(0, 1), (1, 0)]) for swap in swaps]
    parts = [add(pair) for pair in zip(keeps, others)]
    for swapped in range(2):
        terms = [parts[0], *[around(parts[s], s, swapped) for s in range(1, RING)]]
        group = max(terms[0].shape[0] // RING, 2)
        parts = [add([term[j : j + group] for term in terms]) for j in range(0, terms[0].shape[0], group)]
    total = parts[0]
    core = lax.axis_index("c") == 0
    mine = jnp.where(core, total[:1], total[1:])
    theirs = lax.ppermute(jnp.where(core, total[1:], total[:1]), "c", [(0, 1), (1, 0)])
    first, second = jnp.where(core, mine, theirs), jnp.where(core, theirs, mine)
    return (rows, jnp.concatenate([first, second], axis=0))


def solution(mesh):
    fine = Mesh(mesh.devices.reshape(4, 4, 4, 2), AXES)
    placed = tuple(P(AXES, *[None] * extra) for extra in (3, 1, 1, 2, 3, 2, 1, 1, 2))
    return jax.shard_map(
        body,
        mesh=fine,
        in_specs=placed,
        out_specs=(P(AXES, None, None, None), P(AXES, None, None)),
        check_vma=False,
    )
```

```python
import jax
import jax.numpy as jnp
from jax import lax
from jax.experimental import pallas as pl
from jax.experimental.pallas import tpu as pltpu
from jax.sharding import Mesh
from jax.sharding import PartitionSpec as P

AXES = ("gx", "x", "y", "c")
GY = ("x", "y", "c")
LINKS = 6
LOCAL = 2
BLOCKS = 2
RING = 4
ANY = pl.BlockSpec(memory_space=pl.ANY)
VMEM = pl.BlockSpec(memory_space=pltpu.VMEM)
HBM = pl.BlockSpec(memory_space=pltpu.HBM)
SMEM = pl.BlockSpec(memory_space=pltpu.SMEM)
PARAMS = pltpu.CompilerParams(vmem_limit_bytes=26 << 20)


def shifted(value, axis, steps):
    count = lax.axis_size(axis)
    first, last = (max(0, -steps), min(count, count - steps))
    return lax.ppermute(value, axis, [(source, source + steps) for source in range(first, last)])


def around(value, steps, swapped):
    pairs = []
    for x in range(RING):
        for y in range(RING):
            for c in range(2):
                to_x, to_y = ((x + steps) % RING, y) if c == swapped else (x, (y + steps) % RING)
                pairs.append(((x * RING + y) * 2 + c, (to_x * RING + to_y) * 2 + c))
    return lax.ppermute(value, GY, pairs)


def shape(*sizes):
    return jax.ShapeDtypeStruct(sizes, jnp.bfloat16)


def pick_kernel(slab, rows_ref, up_ref, down_ref, held, sems):
    arrivals = [pltpu.make_async_copy(rows_ref.at[slab[0, j]], held.at[j], sems.at[j]) for j in range(2)]
    copies = [pltpu.make_async_copy(held.at[j], out.at[0], sems.at[2 + j]) for j, out in enumerate((up_ref, down_ref))]
    for copy in arrivals:
        copy.start()
    for arrival, copy in zip(arrivals, copies):
        arrival.wait()
        copy.start()
    for copy in copies:
        copy.wait()


def pick(slab, rows):
    one = shape(1, *rows.shape[1:])
    return pl.pallas_call(
        pick_kernel,
        in_specs=[SMEM, ANY],
        out_specs=[ANY, ANY],
        out_shape=(one, one),
        scratch_shapes=[pltpu.VMEM((2, *rows.shape[1:]), jnp.bfloat16), pltpu.SemaphoreType.DMA((4,))],
        compiler_params=PARAMS,
        name="pick_rows",
    )(slab, rows)


def pack_kernel(peer, rows_ref, out_ref, own, in_sems, sems):
    arrivals = [pltpu.make_async_copy(rows_ref.at[j], own.at[j], in_sems.at[j]) for j in range(own.shape[0])]
    for copy in arrivals:
        copy.start()
    for copy in arrivals:
        copy.wait()
    copies = [pltpu.make_async_copy(own.at[peer[0, q]], out_ref.at[q], sems.at[q]) for q in range(out_ref.shape[0])]
    for copy in copies:
        copy.start()
    for copy in copies:
        copy.wait()


def pack(peer, rows):
    peers = peer.shape[1]
    return pl.pallas_call(
        pack_kernel,
        in_specs=[SMEM, ANY],
        out_specs=ANY,
        out_shape=shape(peers, *rows.shape[1:]),
        scratch_shapes=[
            pltpu.VMEM(rows.shape, jnp.bfloat16),
            pltpu.SemaphoreType.DMA((rows.shape[0],)),
            pltpu.SemaphoreType.DMA((peers,)),
        ],
        cost_estimate=pl.CostEstimate(flops=0, transcendentals=0, bytes_accessed=10 << 20),
        compiler_params=PARAMS,
        name="pack_rows",
    )(peer, rows)


def row_image(local, remote, match, i, a_buf, own, peers, low, high, rhs):
    width = own.shape[-1]
    first, count = own.shape[0], peers.shape[0]
    for k in range(LINKS):
        for n in range(BLOCKS):
            wanted = match[k, n, i]
            there = jnp.minimum(wanted, BLOCKS - 1)
            if k < LOCAL:
                block = own[local[k, i], there]
            else:
                column = remote[k - LOCAL, i]
                block = peers[jnp.clip(column - first, 0, count - 1), there]
                block = jnp.where(column == first + count, low[0, there], block)
                block = jnp.where(column > first + count, high[0, there], block)
            block = jnp.where(wanted < BLOCKS, block, jnp.zeros_like(block))
            rhs[k * width : (k + 1) * width, n * width : (n + 1) * width] = block
    lhs = jnp.concatenate([a_buf[i, k] for k in range(LINKS)], axis=1)
    return jnp.dot(lhs, rhs[...], preferred_element_type=jnp.float32).astype(jnp.bfloat16)


def new_row(local, remote, match, i, a_buf, d_buf, own, peers, low, high, rhs):
    width = own.shape[-1]
    image = row_image(local, remote, match, i, a_buf, own, peers, low, high, rhs)
    update = jnp.dot(d_buf[i], image, preferred_element_type=jnp.float32)
    halves = [update[:, n * width : (n + 1) * width] for n in range(BLOCKS)]
    return [(own[i, n].astype(jnp.float32) - halves[n]).astype(jnp.bfloat16) for n in range(BLOCKS)]


def slab_kernel(
    local, remote, match, slab,
    a_buf, d_buf, own, peers, low, high,
    up, down,
    rhs,
):
    for j, out in enumerate((up, down)):
        for n, value in enumerate(new_row(local, remote, match, slab[0, j], a_buf, d_buf, own, peers, low, high, rhs)):
            out[0, n] = value


def smooth_kernel(
    local, remote, match, peer,
    a_buf, d_buf, own, peers, low, high,
    new, out_hbm,
    rhs,
    out_sem,
):
    @pl.loop(0, own.shape[0])
    def _(i):
        for n, value in enumerate(new_row(local, remote, match, i, a_buf, d_buf, own, peers, low, high, rhs)):
            new[i, n] = value
        for q in range(out_hbm.shape[0]):

            @pl.when(peer[0, q] == i)
            def _():
                pltpu.make_async_copy(new.at[i], out_hbm.at[q], out_sem.at[0]).start()

    pltpu.make_async_copy(out_hbm, out_hbm, out_sem.at[0]).wait()


def operand_scratch(width):
    return pltpu.VMEM((LINKS * width, BLOCKS * width), jnp.bfloat16)


def slab_rows(tables, slab, operator, inverse, rows, received, low, high):
    width = operator.shape[-1]
    one = shape(1, *rows.shape[1:])
    return pl.pallas_call(
        slab_kernel,
        in_specs=[SMEM] * 4 + [VMEM] * 6,
        out_specs=[VMEM] * 2,
        out_shape=(one, one),
        scratch_shapes=[operand_scratch(width)],
        compiler_params=PARAMS,
        name="slab_rows",
    )(*tables, slab, operator, inverse, rows, received, low, high)


def smooth(tables, peer, operator, inverse, rows, received, low, high):
    count, _, width, _ = operator.shape
    flops = 2 * count * (LINKS + 1) * BLOCKS * width**3
    return pl.pallas_call(
        smooth_kernel,
        in_specs=[SMEM] * 4 + [VMEM] * 6,
        out_specs=[VMEM, HBM],
        out_shape=(shape(*rows.shape), shape(*received.shape)),
        scratch_shapes=[operand_scratch(width), pltpu.SemaphoreType.DMA((1,))],
        cost_estimate=pl.CostEstimate(flops=flops, transcendentals=0, bytes_accessed=28 << 20),
        compiler_params=PARAMS,
        name="smooth_rows",
    )(*tables, peer, operator, inverse, rows, received, low, high)


def galerkin_kernel(
    local, remote, match, slots, here,
    a_buf, own, peers, low, high,
    sums,
    rhs,
):
    width = own.shape[-1]
    sums[...] = jnp.zeros_like(sums)

    @pl.loop(0, own.shape[0])
    def _(i):
        image = row_image(local, remote, match, i, a_buf, own, peers, low, high, rhs)
        mine = jnp.concatenate([own[i, n] for n in range(BLOCKS)], axis=1)
        partial = lax.dot_general(mine, image, (((0,), (0,)), ((), ())), preferred_element_type=jnp.float32)
        for n1 in range(BLOCKS):
            for n2 in range(BLOCKS):
                slot = slots[n1, n2, i]
                owner = slot // 2
                chip = owner // 2
                dx = (chip // RING - here[0] + RING) % RING
                dy = (chip % RING - here[1] + RING) % RING
                second = slot % 2
                step = jnp.where(second == 0, dx, dy)
                place = jnp.where(second == 0, dy, dx) * 2 + owner % 2
                group = jnp.where(second == here[2], 0, RING) + step
                block = partial[n1 * width : (n1 + 1) * width, n2 * width : (n2 + 1) * width]
                sums[group, place] = block.astype(jnp.bfloat16)


def galerkin(tables, slots, here, operator, rows, received, low, high):
    width = operator.shape[-1]
    return pl.pallas_call(
        galerkin_kernel,
        in_specs=[SMEM] * 5 + [VMEM] * 5,
        out_specs=VMEM,
        out_shape=shape(2 * RING, 2 * RING, width, width),
        scratch_shapes=[operand_scratch(width)],
        compiler_params=PARAMS,
        name="galerkin_rows",
    )(*tables, slots, here, operator, rows, received, low, high)


def add(terms):
    total = terms[0].astype(jnp.float32)
    for term in terms[1:]:
        total = total + term.astype(jnp.float32)
    return total.astype(jnp.bfloat16)


def body(
    operator_blocks,
    local_columns,
    remote_columns,
    match_slots,
    tentative,
    inverse_diagonal,
    peer,
    slab,
    coarse_slots,
):
    tables = (local_columns.T, remote_columns.T, match_slots.transpose(1, 2, 0))
    slots = coarse_slots.transpose(1, 2, 0)
    here = jnp.stack([lax.axis_index("x"), lax.axis_index("y"), lax.axis_index("c")]).astype(jnp.int32)
    rows = tentative
    up, down = pick(slab, rows)
    low, high = shifted(up, "gx", 1), shifted(down, "gx", -1)
    outgoing = pack(peer, rows)
    outgoing, low, high, here = lax.optimization_barrier((outgoing, low, high, here))
    received = lax.all_to_all(outgoing, GY, split_axis=0, concat_axis=0, tiled=True)
    for smooth_pass in range(2):
        operands = (operator_blocks, inverse_diagonal, rows, received, low, high)
        up, down = slab_rows(tables, slab, *operands)
        up, down, operands = lax.optimization_barrier((up, down, operands))
        low, high = shifted(up, "gx", 1), shifted(down, "gx", -1)
        rows, outgoing = smooth(tables, peer, *operands)
        outgoing, low, high = lax.optimization_barrier((outgoing, low, high))
        received = lax.all_to_all(outgoing, GY, split_axis=0, concat_axis=0, tiled=True)
    sums = galerkin(tables, slots, here, operator_blocks, rows, received, low, high)
    others = [lax.ppermute(sums[RING + j], "c", [(0, 1), (1, 0)]) for j in range(RING)]
    parts = [None] * RING
    ready = None
    for j in (1, 2, 3, 0):
        other = others[j]
        if ready is not None:
            other, parts[ready] = lax.optimization_barrier((other, parts[ready]))
        parts[j] = add((sums[j], other))
        ready = j
    for swapped in range(2):
        terms = [parts[0], *[around(parts[s], s, swapped) for s in range(1, RING)]]
        group = max(terms[0].shape[0] // RING, 2)
        parts = [add([term[j : j + group] for term in terms]) for j in range(0, terms[0].shape[0], group)]
    total = parts[0]
    core = lax.axis_index("c") == 0
    mine = jnp.where(core, total[:1], total[1:])
    theirs = lax.ppermute(jnp.where(core, total[1:], total[:1]), "c", [(0, 1), (1, 0)])
    first, second = jnp.where(core, mine, theirs), jnp.where(core, theirs, mine)
    return (rows, jnp.concatenate([first, second], axis=0))


def solution(mesh):
    fine = Mesh(mesh.devices.reshape(4, 4, 4, 2), AXES)
    placed = tuple(P(AXES, *[None] * extra) for extra in (3, 1, 1, 2, 3, 2, 1, 1, 2))
    return jax.shard_map(
        body,
        mesh=fine,
        in_specs=placed,
        out_specs=(P(AXES, None, None, None), P(AXES, None, None)),
        check_vma=False,
    )
```

```python
import jax
import jax.numpy as jnp
from jax import lax
from jax.experimental import pallas as pl
from jax.experimental.pallas import tpu as pltpu
from jax.sharding import Mesh
from jax.sharding import PartitionSpec as P

AXES = ("gx", "x", "y", "c")
GY = ("x", "y", "c")
LINKS = 6
LOCAL = 2
BLOCKS = 2
RING = 4
ANY = pl.BlockSpec(memory_space=pl.ANY)
VMEM = pl.BlockSpec(memory_space=pltpu.VMEM)
SMEM = pl.BlockSpec(memory_space=pltpu.SMEM)
PARAMS = pltpu.CompilerParams(vmem_limit_bytes=26 << 20)


def shifted(value, axis, steps):
    count = lax.axis_size(axis)
    first, last = (max(0, -steps), min(count, count - steps))
    return lax.ppermute(value, axis, [(source, source + steps) for source in range(first, last)])


def around(value, steps, swapped):
    pairs = []
    for x in range(RING):
        for y in range(RING):
            for c in range(2):
                to_x, to_y = ((x + steps) % RING, y) if c == swapped else (x, (y + steps) % RING)
                pairs.append(((x * RING + y) * 2 + c, (to_x * RING + to_y) * 2 + c))
    return lax.ppermute(value, GY, pairs)


def shape(*sizes):
    return jax.ShapeDtypeStruct(sizes, jnp.bfloat16)


def pick_kernel(slab, rows_ref, up_ref, down_ref, held, sems):
    arrivals = [pltpu.make_async_copy(rows_ref.at[slab[0, j]], held.at[j], sems.at[j]) for j in range(2)]
    copies = [pltpu.make_async_copy(held.at[j], out.at[0], sems.at[2 + j]) for j, out in enumerate((up_ref, down_ref))]
    for copy in arrivals:
        copy.start()
    for arrival, copy in zip(arrivals, copies):
        arrival.wait()
        copy.start()
    for copy in copies:
        copy.wait()


def pick(slab, rows):
    one = shape(1, *rows.shape[1:])
    return pl.pallas_call(
        pick_kernel,
        in_specs=[SMEM, ANY],
        out_specs=[ANY, ANY],
        out_shape=(one, one),
        scratch_shapes=[pltpu.VMEM((2, *rows.shape[1:]), jnp.bfloat16), pltpu.SemaphoreType.DMA((4,))],
        compiler_params=PARAMS,
        name="pick_rows",
    )(slab, rows)


def pack_kernel(peer, rows_ref, out_ref, own, in_sems, sems):
    arrivals = [pltpu.make_async_copy(rows_ref.at[j], own.at[j], in_sems.at[j]) for j in range(own.shape[0])]
    for copy in arrivals:
        copy.start()
    for copy in arrivals:
        copy.wait()
    copies = [pltpu.make_async_copy(own.at[peer[0, q]], out_ref.at[q], sems.at[q]) for q in range(out_ref.shape[0])]
    for copy in copies:
        copy.start()
    for copy in copies:
        copy.wait()


def pack(peer, rows):
    peers = peer.shape[1]
    return pl.pallas_call(
        pack_kernel,
        in_specs=[SMEM, ANY],
        out_specs=ANY,
        out_shape=shape(peers, *rows.shape[1:]),
        scratch_shapes=[
            pltpu.VMEM(rows.shape, jnp.bfloat16),
            pltpu.SemaphoreType.DMA((rows.shape[0],)),
            pltpu.SemaphoreType.DMA((peers,)),
        ],
        cost_estimate=pl.CostEstimate(flops=0, transcendentals=0, bytes_accessed=10 << 20),
        compiler_params=PARAMS,
        name="pack_rows",
    )(peer, rows)


def row_image(local, remote, match, i, a_buf, own, peers, low, high, rhs):
    width = own.shape[-1]
    first, count = own.shape[0], peers.shape[0]
    for k in range(LINKS):
        for n in range(BLOCKS):
            wanted = match[k, n, i]
            there = jnp.minimum(wanted, BLOCKS - 1)
            if k < LOCAL:
                block = own[local[k, i], there]
            else:
                column = remote[k - LOCAL, i]
                block = peers[jnp.clip(column - first, 0, count - 1), there]
                block = jnp.where(column == first + count, low[0, there], block)
                block = jnp.where(column > first + count, high[0, there], block)
            block = jnp.where(wanted < BLOCKS, block, jnp.zeros_like(block))
            rhs[k * width : (k + 1) * width, n * width : (n + 1) * width] = block
    lhs = jnp.concatenate([a_buf[i, k] for k in range(LINKS)], axis=1)
    return jnp.dot(lhs, rhs[...], preferred_element_type=jnp.float32).astype(jnp.bfloat16)


def new_row(local, remote, match, i, a_buf, d_buf, own, peers, low, high, rhs):
    width = own.shape[-1]
    image = row_image(local, remote, match, i, a_buf, own, peers, low, high, rhs)
    update = jnp.dot(d_buf[i], image, preferred_element_type=jnp.float32)
    halves = [update[:, n * width : (n + 1) * width] for n in range(BLOCKS)]
    return [(own[i, n].astype(jnp.float32) - halves[n]).astype(jnp.bfloat16) for n in range(BLOCKS)]


def slab_kernel(
    local, remote, match, slab,
    a_buf, d_buf, own, peers, low, high,
    up, down,
    rhs,
):
    for j, out in enumerate((up, down)):
        for n, value in enumerate(new_row(local, remote, match, slab[0, j], a_buf, d_buf, own, peers, low, high, rhs)):
            out[0, n] = value


def smooth_kernel(
    local, remote, match, peer,
    a_buf, d_buf, own, peers, low, high,
    rows_hbm, out_hbm,
    new, rhs,
    rows_sem, out_sems,
):
    @pl.loop(0, own.shape[0])
    def _(i):
        for n, value in enumerate(new_row(local, remote, match, i, a_buf, d_buf, own, peers, low, high, rhs)):
            new[i, n] = value
        pltpu.make_async_copy(new.at[i], rows_hbm.at[i], rows_sem.at[0]).start()

    copies = [pltpu.make_async_copy(new.at[peer[0, q]], out_hbm.at[q], out_sems.at[q]) for q in range(out_hbm.shape[0])]
    for copy in copies:
        copy.start()
    pltpu.make_async_copy(rows_hbm, rows_hbm, rows_sem.at[0]).wait()
    for copy in copies:
        copy.wait()


def operand_scratch(width):
    return pltpu.VMEM((LINKS * width, BLOCKS * width), jnp.bfloat16)


def slab_rows(tables, slab, operator, inverse, rows, received, low, high):
    width = operator.shape[-1]
    one = shape(1, *rows.shape[1:])
    return pl.pallas_call(
        slab_kernel,
        in_specs=[SMEM] * 4 + [VMEM] * 6,
        out_specs=[VMEM] * 2,
        out_shape=(one, one),
        scratch_shapes=[operand_scratch(width)],
        compiler_params=PARAMS,
        name="slab_rows",
    )(*tables, slab, operator, inverse, rows, received, low, high)


def smooth(tables, peer, operator, inverse, rows, received, low, high):
    count, _, width, _ = operator.shape
    flops = 2 * count * (LINKS + 1) * BLOCKS * width**3
    return pl.pallas_call(
        smooth_kernel,
        in_specs=[SMEM] * 4 + [VMEM] * 6,
        out_specs=[ANY, ANY],
        out_shape=(shape(*rows.shape), shape(*received.shape)),
        scratch_shapes=[
            pltpu.VMEM(rows.shape, jnp.bfloat16),
            operand_scratch(width),
            pltpu.SemaphoreType.DMA((1,)),
            pltpu.SemaphoreType.DMA((received.shape[0],)),
        ],
        cost_estimate=pl.CostEstimate(flops=flops, transcendentals=0, bytes_accessed=28 << 20),
        compiler_params=PARAMS,
        name="smooth_rows",
    )(*tables, peer, operator, inverse, rows, received, low, high)


def galerkin_kernel(
    local, remote, match, slots, here,
    a_buf, own, peers, low, high,
    sums,
    rhs,
):
    width = own.shape[-1]
    sums[...] = jnp.zeros_like(sums)

    @pl.loop(0, own.shape[0])
    def _(i):
        image = row_image(local, remote, match, i, a_buf, own, peers, low, high, rhs)
        mine = jnp.concatenate([own[i, n] for n in range(BLOCKS)], axis=1)
        partial = lax.dot_general(mine, image, (((0,), (0,)), ((), ())), preferred_element_type=jnp.float32)
        for n1 in range(BLOCKS):
            for n2 in range(BLOCKS):
                slot = slots[n1, n2, i]
                owner = slot // 2
                chip = owner // 2
                dx = (chip // RING - here[0] + RING) % RING
                dy = (chip % RING - here[1] + RING) % RING
                second = slot % 2
                step = jnp.where(second == 0, dx, dy)
                place = jnp.where(second == 0, dy, dx) * 2 + owner % 2
                group = jnp.where(second == here[2], 0, RING) + step
                block = partial[n1 * width : (n1 + 1) * width, n2 * width : (n2 + 1) * width]
                sums[group, place] = block.astype(jnp.bfloat16)


def galerkin(tables, slots, here, operator, rows, received, low, high):
    width = operator.shape[-1]
    return pl.pallas_call(
        galerkin_kernel,
        in_specs=[SMEM] * 5 + [VMEM] * 5,
        out_specs=VMEM,
        out_shape=shape(2 * RING, 2 * RING, width, width),
        scratch_shapes=[operand_scratch(width)],
        compiler_params=PARAMS,
        name="galerkin_rows",
    )(*tables, slots, here, operator, rows, received, low, high)


def add(terms):
    total = terms[0].astype(jnp.float32)
    for term in terms[1:]:
        total = total + term.astype(jnp.float32)
    return total.astype(jnp.bfloat16)


def body(
    operator_blocks,
    local_columns,
    remote_columns,
    match_slots,
    tentative,
    inverse_diagonal,
    peer,
    slab,
    coarse_slots,
):
    tables = (local_columns.T, remote_columns.T, match_slots.transpose(1, 2, 0))
    slots = coarse_slots.transpose(1, 2, 0)
    here = jnp.stack([lax.axis_index("x"), lax.axis_index("y"), lax.axis_index("c")]).astype(jnp.int32)
    rows = tentative
    up, down = pick(slab, rows)
    low, high = shifted(up, "gx", 1), shifted(down, "gx", -1)
    outgoing = pack(peer, rows)
    outgoing, low, high, here = lax.optimization_barrier((outgoing, low, high, here))
    received = lax.all_to_all(outgoing, GY, split_axis=0, concat_axis=0, tiled=True)
    for smooth_pass in range(2):
        operands = (operator_blocks, inverse_diagonal, rows, received, low, high)
        up, down = slab_rows(tables, slab, *operands)
        up, down, operands = lax.optimization_barrier((up, down, operands))
        low, high = shifted(up, "gx", 1), shifted(down, "gx", -1)
        rows, outgoing = smooth(tables, peer, *operands)
        outgoing, low, high = lax.optimization_barrier((outgoing, low, high))
        received = lax.all_to_all(outgoing, GY, split_axis=0, concat_axis=0, tiled=True)
    sums = galerkin(tables, slots, here, operator_blocks, rows, received, low, high)
    others = [lax.ppermute(sums[RING + j], "c", [(0, 1), (1, 0)]) for j in range(RING)]
    parts = [None] * RING
    ready = None
    for j in (1, 2, 3, 0):
        other = others[j]
        if ready is not None:
            other, parts[ready] = lax.optimization_barrier((other, parts[ready]))
        parts[j] = add((sums[j], other))
        ready = j
    for swapped in range(2):
        terms = [parts[0], *[around(parts[s], s, swapped) for s in range(1, RING)]]
        group = max(terms[0].shape[0] // RING, 2)
        parts = [add([term[j : j + group] for term in terms]) for j in range(0, terms[0].shape[0], group)]
        parts = lax.optimization_barrier(parts)
    total = parts[0]
    core = lax.axis_index("c") == 0
    mine = jnp.where(core, total[:1], total[1:])
    theirs = lax.ppermute(jnp.where(core, total[1:], total[:1]), "c", [(0, 1), (1, 0)])
    first, second = jnp.where(core, mine, theirs), jnp.where(core, theirs, mine)
    return (rows, jnp.concatenate([first, second], axis=0))


def solution(mesh):
    fine = Mesh(mesh.devices.reshape(4, 4, 4, 2), AXES)
    placed = tuple(P(AXES, *[None] * extra) for extra in (3, 1, 1, 2, 3, 2, 1, 1, 2))
    return jax.shard_map(
        body,
        mesh=fine,
        in_specs=placed,
        out_specs=(P(AXES, None, None, None), P(AXES, None, None)),
        check_vma=False,
    )
```

```python
import jax
import jax.numpy as jnp
from jax import lax
from jax.experimental import pallas as pl
from jax.experimental.pallas import tpu as pltpu
from jax.sharding import Mesh
from jax.sharding import PartitionSpec as P

AXES = ("gx", "x", "y", "c")
GY = ("x", "y", "c")
LINKS = 6
LOCAL = 2
BLOCKS = 2
RING = 4
ANY = pl.BlockSpec(memory_space=pl.ANY)
VMEM = pl.BlockSpec(memory_space=pltpu.VMEM)
SMEM = pl.BlockSpec(memory_space=pltpu.SMEM)
PARAMS = pltpu.CompilerParams(vmem_limit_bytes=26 << 20)


def shifted(value, axis, steps):
    count = lax.axis_size(axis)
    first, last = (max(0, -steps), min(count, count - steps))
    return lax.ppermute(value, axis, [(source, source + steps) for source in range(first, last)])


def around(value, steps, swapped):
    pairs = []
    for x in range(RING):
        for y in range(RING):
            for c in range(2):
                to_x, to_y = ((x + steps) % RING, y) if c == swapped else (x, (y + steps) % RING)
                pairs.append(((x * RING + y) * 2 + c, (to_x * RING + to_y) * 2 + c))
    return lax.ppermute(value, GY, pairs)


def shape(*sizes):
    return jax.ShapeDtypeStruct(sizes, jnp.bfloat16)


def pick_kernel(slab, rows_ref, up_ref, down_ref, held, sems):
    arrivals = [pltpu.make_async_copy(rows_ref.at[slab[0, j]], held.at[j], sems.at[j]) for j in range(2)]
    copies = [pltpu.make_async_copy(held.at[j], out.at[0], sems.at[2 + j]) for j, out in enumerate((up_ref, down_ref))]
    for copy in arrivals:
        copy.start()
    for arrival, copy in zip(arrivals, copies):
        arrival.wait()
        copy.start()
    for copy in copies:
        copy.wait()


def pick(slab, rows):
    one = shape(1, *rows.shape[1:])
    return pl.pallas_call(
        pick_kernel,
        in_specs=[SMEM, ANY],
        out_specs=[ANY, ANY],
        out_shape=(one, one),
        scratch_shapes=[pltpu.VMEM((2, *rows.shape[1:]), jnp.bfloat16), pltpu.SemaphoreType.DMA((4,))],
        compiler_params=pltpu.CompilerParams(vmem_limit_bytes=56 << 20),
        name="pick_rows",
    )(slab, rows)


def pack_kernel(peer, rows_ref, out_ref, own, in_sems, sems):
    arrivals = [pltpu.make_async_copy(rows_ref.at[j], own.at[j], in_sems.at[j]) for j in range(own.shape[0])]
    for copy in arrivals:
        copy.start()
    for copy in arrivals:
        copy.wait()
    copies = [pltpu.make_async_copy(own.at[peer[0, q]], out_ref.at[q], sems.at[q]) for q in range(out_ref.shape[0])]
    for copy in copies:
        copy.start()
    for copy in copies:
        copy.wait()


def pack(peer, rows):
    peers = peer.shape[1]
    return pl.pallas_call(
        pack_kernel,
        in_specs=[SMEM, ANY],
        out_specs=ANY,
        out_shape=shape(peers, *rows.shape[1:]),
        scratch_shapes=[
            pltpu.VMEM(rows.shape, jnp.bfloat16),
            pltpu.SemaphoreType.DMA((rows.shape[0],)),
            pltpu.SemaphoreType.DMA((peers,)),
        ],
        cost_estimate=pl.CostEstimate(flops=0, transcendentals=0, bytes_accessed=10 << 20),
        compiler_params=PARAMS,
        name="pack_rows",
    )(peer, rows)


def row_image(local, remote, match, i, a_buf, own, peers, low, high, rhs):
    width = own.shape[-1]
    first, count = own.shape[0], peers.shape[0]
    for k in range(LINKS):
        for n in range(BLOCKS):
            wanted = match[k, n, i]
            there = jnp.minimum(wanted, BLOCKS - 1)
            if k < LOCAL:
                block = own[local[k, i], there]
            else:
                column = remote[k - LOCAL, i]
                block = peers[jnp.clip(column - first, 0, count - 1), there]
                block = jnp.where(column == first + count, low[0, there], block)
                block = jnp.where(column > first + count, high[0, there], block)
            block = jnp.where(wanted < BLOCKS, block, jnp.zeros_like(block))
            rhs[k * width : (k + 1) * width, n * width : (n + 1) * width] = block
    lhs = jnp.concatenate([a_buf[i, k] for k in range(LINKS)], axis=1)
    return jnp.dot(lhs, rhs[...], preferred_element_type=jnp.float32).astype(jnp.bfloat16)


def new_row(local, remote, match, i, a_buf, d_buf, own, peers, low, high, rhs):
    width = own.shape[-1]
    image = row_image(local, remote, match, i, a_buf, own, peers, low, high, rhs)
    update = jnp.dot(d_buf[i], image, preferred_element_type=jnp.float32)
    halves = [update[:, n * width : (n + 1) * width] for n in range(BLOCKS)]
    return [(own[i, n].astype(jnp.float32) - halves[n]).astype(jnp.bfloat16) for n in range(BLOCKS)]


def slab_kernel(
    local, remote, match, slab,
    a_buf, d_buf, own, peers, low, high,
    up, down,
    rhs,
):
    for j, out in enumerate((up, down)):
        for n, value in enumerate(new_row(local, remote, match, slab[0, j], a_buf, d_buf, own, peers, low, high, rhs.at[0])):
            out[0, n] = value


def smooth_kernel(
    local, remote, match, peer,
    a_buf, d_buf, own, peers, low, high,
    rows_hbm, out_hbm,
    new, rhs,
    rows_sem, out_sems,
):
    @pl.loop(0, own.shape[0], step=2)
    def _(start):
        for lane in range(2):
            i = start + lane
            for n, value in enumerate(new_row(local, remote, match, i, a_buf, d_buf, own, peers, low, high, rhs.at[lane])):
                new[i, n] = value
        for lane in range(2):
            pltpu.make_async_copy(new.at[start + lane], rows_hbm.at[start + lane], rows_sem.at[0]).start()

    copies = [pltpu.make_async_copy(new.at[peer[0, q]], out_hbm.at[q], out_sems.at[q]) for q in range(out_hbm.shape[0])]
    for copy in copies:
        copy.start()
    pltpu.make_async_copy(rows_hbm, rows_hbm, rows_sem.at[0]).wait()
    for copy in copies:
        copy.wait()


def operand_scratch(width):
    return pltpu.VMEM((2, LINKS * width, BLOCKS * width), jnp.bfloat16)


def slab_rows(tables, slab, operator, inverse, rows, received, low, high):
    width = operator.shape[-1]
    one = shape(1, *rows.shape[1:])
    return pl.pallas_call(
        slab_kernel,
        in_specs=[SMEM] * 4 + [VMEM] * 6,
        out_specs=[VMEM] * 2,
        out_shape=(one, one),
        scratch_shapes=[operand_scratch(width)],
        compiler_params=PARAMS,
        name="slab_rows",
    )(*tables, slab, operator, inverse, rows, received, low, high)


def smooth(tables, peer, operator, inverse, rows, received, low, high):
    count, _, width, _ = operator.shape
    flops = 2 * count * (LINKS + 1) * BLOCKS * width**3
    return pl.pallas_call(
        smooth_kernel,
        in_specs=[SMEM] * 4 + [VMEM] * 6,
        out_specs=[ANY, ANY],
        out_shape=(shape(*rows.shape), shape(*received.shape)),
        scratch_shapes=[
            pltpu.VMEM(rows.shape, jnp.bfloat16),
            operand_scratch(width),
            pltpu.SemaphoreType.DMA((1,)),
            pltpu.SemaphoreType.DMA((received.shape[0],)),
        ],
        cost_estimate=pl.CostEstimate(flops=flops, transcendentals=0, bytes_accessed=28 << 20),
        compiler_params=PARAMS,
        name="smooth_rows",
    )(*tables, peer, operator, inverse, rows, received, low, high)


def galerkin_kernel(
    local, remote, match, slots, here,
    a_buf, own, peers, low, high,
    sums,
    rhs,
):
    width = own.shape[-1]
    sums[...] = jnp.zeros_like(sums)

    @pl.loop(0, own.shape[0], step=2)
    def _(start):
        for lane in range(2):
            i = start + lane
            image = row_image(local, remote, match, i, a_buf, own, peers, low, high, rhs.at[lane])
            mine = jnp.concatenate([own[i, n] for n in range(BLOCKS)], axis=1)
            partial = lax.dot_general(mine, image, (((0,), (0,)), ((), ())), preferred_element_type=jnp.float32)
            for n1 in range(BLOCKS):
                for n2 in range(BLOCKS):
                    slot = slots[n1, n2, i]
                    owner = slot // 2
                    chip = owner // 2
                    dx = (chip // RING - here[0] + RING) % RING
                    dy = (chip % RING - here[1] + RING) % RING
                    second = slot % 2
                    step = jnp.where(second == 0, dx, dy)
                    place = jnp.where(second == 0, dy, dx) * 2 + owner % 2
                    group = jnp.where(second == here[2], 0, RING) + step
                    block = partial[n1 * width : (n1 + 1) * width, n2 * width : (n2 + 1) * width]
                    sums[group, place] = block.astype(jnp.bfloat16)


def galerkin(tables, slots, here, operator, rows, received, low, high):
    width = operator.shape[-1]
    return pl.pallas_call(
        galerkin_kernel,
        in_specs=[SMEM] * 5 + [VMEM] * 5,
        out_specs=VMEM,
        out_shape=shape(2 * RING, 2 * RING, width, width),
        scratch_shapes=[operand_scratch(width)],
        compiler_params=PARAMS,
        name="galerkin_rows",
    )(*tables, slots, here, operator, rows, received, low, high)


def add(terms):
    total = terms[0].astype(jnp.float32)
    for term in terms[1:]:
        total = total + term.astype(jnp.float32)
    return total.astype(jnp.bfloat16)


def body(
    operator_blocks,
    local_columns,
    remote_columns,
    match_slots,
    tentative,
    inverse_diagonal,
    peer,
    slab,
    coarse_slots,
):
    tables = (local_columns.T, remote_columns.T, match_slots.transpose(1, 2, 0))
    slots = coarse_slots.transpose(1, 2, 0)
    here = jnp.stack([lax.axis_index("x"), lax.axis_index("y"), lax.axis_index("c")]).astype(jnp.int32)
    rows = tentative
    up, down = pick(slab, rows)
    low, high = shifted(up, "gx", 1), shifted(down, "gx", -1)
    outgoing = pack(peer, rows)
    outgoing, low, high, here = lax.optimization_barrier((outgoing, low, high, here))
    received = lax.all_to_all(outgoing, GY, split_axis=0, concat_axis=0, tiled=True)
    for smooth_pass in range(2):
        operands = (operator_blocks, inverse_diagonal, rows, received, low, high)
        up, down = slab_rows(tables, slab, *operands)
        up, down, operands = lax.optimization_barrier((up, down, operands))
        low, high = shifted(up, "gx", 1), shifted(down, "gx", -1)
        rows, outgoing = smooth(tables, peer, *operands)
        outgoing, low, high = lax.optimization_barrier((outgoing, low, high))
        received = lax.all_to_all(outgoing, GY, split_axis=0, concat_axis=0, tiled=True)
    sums = galerkin(tables, slots, here, operator_blocks, rows, received, low, high)
    others = [lax.ppermute(sums[RING + j], "c", [(0, 1), (1, 0)]) for j in range(RING)]
    parts = [None] * RING
    ready = None
    for j in (1, 2, 3, 0):
        other = others[j]
        if ready is not None:
            other, parts[ready] = lax.optimization_barrier((other, parts[ready]))
        parts[j] = add((sums[j], other))
        ready = j
    for swapped in range(2):
        terms = [parts[0], *[around(parts[s], s, swapped) for s in range(1, RING)]]
        group = max(terms[0].shape[0] // RING, 2)
        parts = [add([term[j : j + group] for term in terms]) for j in range(0, terms[0].shape[0], group)]
        parts = lax.optimization_barrier(parts)
    total = parts[0]
    core = lax.axis_index("c") == 0
    mine = jnp.where(core, total[:1], total[1:])
    theirs = lax.ppermute(jnp.where(core, total[1:], total[:1]), "c", [(0, 1), (1, 0)])
    first, second = jnp.where(core, mine, theirs), jnp.where(core, theirs, mine)
    return (rows, jnp.concatenate([first, second], axis=0))


def solution(mesh):
    fine = Mesh(mesh.devices.reshape(4, 4, 4, 2), AXES)
    placed = tuple(P(AXES, *[None] * extra) for extra in (3, 1, 1, 2, 3, 2, 1, 1, 2))
    return jax.shard_map(
        body,
        mesh=fine,
        in_specs=placed,
        out_specs=(P(AXES, None, None, None), P(AXES, None, None)),
        check_vma=False,
    )
```

```python
import jax
import jax.numpy as jnp
from jax import lax
from jax.experimental import pallas as pl
from jax.experimental.pallas import tpu as pltpu
from jax.sharding import Mesh
from jax.sharding import PartitionSpec as P

AXES = ("gx", "x", "y", "c")
GY = ("x", "y", "c")
LINKS = 6
LOCAL = 2
BLOCKS = 2
RING = 4
ANY = pl.BlockSpec(memory_space=pl.ANY)
VMEM = pl.BlockSpec(memory_space=pltpu.VMEM)
SMEM = pl.BlockSpec(memory_space=pltpu.SMEM)
PARAMS = pltpu.CompilerParams(vmem_limit_bytes=26 << 20)


def shifted(value, axis, steps):
    count = lax.axis_size(axis)
    first, last = (max(0, -steps), min(count, count - steps))
    return lax.ppermute(value, axis, [(source, source + steps) for source in range(first, last)])


def around(value, steps, swapped):
    pairs = []
    for x in range(RING):
        for y in range(RING):
            for c in range(2):
                to_x, to_y = ((x + steps) % RING, y) if c == swapped else (x, (y + steps) % RING)
                pairs.append(((x * RING + y) * 2 + c, (to_x * RING + to_y) * 2 + c))
    return lax.ppermute(value, GY, pairs)


def shape(*sizes):
    return jax.ShapeDtypeStruct(sizes, jnp.bfloat16)


def pick_kernel(slab, rows_ref, up_ref, down_ref, held, sems):
    arrivals = [pltpu.make_async_copy(rows_ref.at[slab[0, j]], held.at[j], sems.at[j]) for j in range(2)]
    copies = [pltpu.make_async_copy(held.at[j], out.at[0], sems.at[2 + j]) for j, out in enumerate((up_ref, down_ref))]
    for copy in arrivals:
        copy.start()
    for arrival, copy in zip(arrivals, copies):
        arrival.wait()
        copy.start()
    for copy in copies:
        copy.wait()


def pick(slab, rows):
    one = shape(1, *rows.shape[1:])
    return pl.pallas_call(
        pick_kernel,
        in_specs=[SMEM, ANY],
        out_specs=[ANY, ANY],
        out_shape=(one, one),
        scratch_shapes=[pltpu.VMEM((2, *rows.shape[1:]), jnp.bfloat16), pltpu.SemaphoreType.DMA((4,))],
        compiler_params=pltpu.CompilerParams(vmem_limit_bytes=56 << 20),
        name="pick_rows",
    )(slab, rows)


def pack_kernel(peer, rows_ref, out_ref, own, in_sems, sems):
    arrivals = [pltpu.make_async_copy(rows_ref.at[j], own.at[j], in_sems.at[j]) for j in range(own.shape[0])]
    for copy in arrivals:
        copy.start()
    for copy in arrivals:
        copy.wait()
    copies = [pltpu.make_async_copy(own.at[peer[0, q]], out_ref.at[q], sems.at[q]) for q in range(out_ref.shape[0])]
    for copy in copies:
        copy.start()
    for copy in copies:
        copy.wait()


def pack(peer, rows):
    peers = peer.shape[1]
    return pl.pallas_call(
        pack_kernel,
        in_specs=[SMEM, ANY],
        out_specs=ANY,
        out_shape=shape(peers, *rows.shape[1:]),
        scratch_shapes=[
            pltpu.VMEM(rows.shape, jnp.bfloat16),
            pltpu.SemaphoreType.DMA((rows.shape[0],)),
            pltpu.SemaphoreType.DMA((peers,)),
        ],
        cost_estimate=pl.CostEstimate(flops=0, transcendentals=0, bytes_accessed=10 << 20),
        compiler_params=PARAMS,
        name="pack_rows",
    )(peer, rows)


def row_image(local, remote, match, i, a_buf, own, peers, low, high, rhs):
    width = own.shape[-1]
    first, count = own.shape[0], peers.shape[0]
    for k in range(LINKS):
        for n in range(BLOCKS):
            wanted = match[k, n, i]
            there = jnp.minimum(wanted, BLOCKS - 1)
            if k < LOCAL:
                block = own[local[k, i], there]
            else:
                column = remote[k - LOCAL, i]
                block = peers[jnp.clip(column - first, 0, count - 1), there]
                block = jnp.where(column == first + count, low[0, there], block)
                block = jnp.where(column > first + count, high[0, there], block)
            block = jnp.where(wanted < BLOCKS, block, jnp.zeros_like(block))
            rhs[k * width : (k + 1) * width, n * width : (n + 1) * width] = block
    lhs = jnp.concatenate([a_buf[i, k] for k in range(LINKS)], axis=1)
    return jnp.dot(lhs, rhs[...], preferred_element_type=jnp.float32).astype(jnp.bfloat16)


def new_row(local, remote, match, i, a_buf, d_buf, own, peers, low, high, rhs):
    width = own.shape[-1]
    image = row_image(local, remote, match, i, a_buf, own, peers, low, high, rhs)
    update = jnp.dot(d_buf[i], image, preferred_element_type=jnp.float32)
    halves = [update[:, n * width : (n + 1) * width] for n in range(BLOCKS)]
    return [(own[i, n].astype(jnp.float32) - halves[n]).astype(jnp.bfloat16) for n in range(BLOCKS)]


def slab_kernel(
    local, remote, match, slab,
    a_buf, d_buf, own, peers, low, high,
    up, down,
    rhs,
):
    for j, out in enumerate((up, down)):
        for n, value in enumerate(new_row(local, remote, match, slab[0, j], a_buf, d_buf, own, peers, low, high, rhs.at[0])):
            out[0, n] = value


def smooth_kernel(
    local, remote, match, peer,
    a_buf, d_buf, own, peers, low, high,
    rows_hbm, out_hbm,
    new, rhs,
    rows_sem, out_sems,
):
    @pl.loop(0, own.shape[0], step=2)
    def _(start):
        for lane in range(2):
            i = start + lane
            for n, value in enumerate(new_row(local, remote, match, i, a_buf, d_buf, own, peers, low, high, rhs.at[lane])):
                new[i, n] = value
        for lane in range(2):
            pltpu.make_async_copy(new.at[start + lane], rows_hbm.at[start + lane], rows_sem.at[0]).start()

    copies = [pltpu.make_async_copy(new.at[peer[0, q]], out_hbm.at[q], out_sems.at[q]) for q in range(out_hbm.shape[0])]
    for copy in copies:
        copy.start()
    pltpu.make_async_copy(rows_hbm, rows_hbm, rows_sem.at[0]).wait()
    for copy in copies:
        copy.wait()


def operand_scratch(width):
    return pltpu.VMEM((2, LINKS * width, BLOCKS * width), jnp.bfloat16)


def slab_rows(tables, slab, operator, inverse, rows, received, low, high):
    width = operator.shape[-1]
    one = shape(1, *rows.shape[1:])
    return pl.pallas_call(
        slab_kernel,
        in_specs=[SMEM] * 4 + [VMEM] * 6,
        out_specs=[VMEM] * 2,
        out_shape=(one, one),
        scratch_shapes=[operand_scratch(width)],
        compiler_params=PARAMS,
        name="slab_rows",
    )(*tables, slab, operator, inverse, rows, received, low, high)


def smooth(tables, peer, operator, inverse, rows, received, low, high):
    count, _, width, _ = operator.shape
    flops = 2 * count * (LINKS + 1) * BLOCKS * width**3
    return pl.pallas_call(
        smooth_kernel,
        in_specs=[SMEM] * 4 + [VMEM] * 6,
        out_specs=[ANY, ANY],
        out_shape=(shape(*rows.shape), shape(*received.shape)),
        scratch_shapes=[
            pltpu.VMEM(rows.shape, jnp.bfloat16),
            operand_scratch(width),
            pltpu.SemaphoreType.DMA((1,)),
            pltpu.SemaphoreType.DMA((received.shape[0],)),
        ],
        cost_estimate=pl.CostEstimate(flops=flops, transcendentals=0, bytes_accessed=28 << 20),
        compiler_params=PARAMS,
        name="smooth_rows",
    )(*tables, peer, operator, inverse, rows, received, low, high)


def galerkin_kernel(
    local, remote, match, slots, here,
    a_buf, own, peers, low, high,
    sums,
    rhs,
):
    width = own.shape[-1]
    sums[...] = jnp.zeros_like(sums)

    @pl.loop(0, own.shape[0], step=2)
    def _(start):
        for lane in range(2):
            i = start + lane
            image = row_image(local, remote, match, i, a_buf, own, peers, low, high, rhs.at[lane])
            mine = jnp.concatenate([own[i, n] for n in range(BLOCKS)], axis=1)
            partial = lax.dot_general(mine, image, (((0,), (0,)), ((), ())), preferred_element_type=jnp.float32)
            for n1 in range(BLOCKS):
                for n2 in range(BLOCKS):
                    slot = slots[n1, n2, i]
                    owner = slot // 2
                    chip = owner // 2
                    dx = (chip // RING - here[0] + RING) % RING
                    dy = (chip % RING - here[1] + RING) % RING
                    second = slot % 2
                    step = jnp.where(second == 0, dx, dy)
                    place = jnp.where(second == 0, dy, dx) * 2 + owner % 2
                    group = jnp.where(second == here[2], 0, RING) + step
                    block = partial[n1 * width : (n1 + 1) * width, n2 * width : (n2 + 1) * width]
                    sums[group, place] = block.astype(jnp.bfloat16)


def galerkin(tables, slots, here, operator, rows, received, low, high):
    width = operator.shape[-1]
    return pl.pallas_call(
        galerkin_kernel,
        in_specs=[SMEM] * 5 + [VMEM] * 5,
        out_specs=VMEM,
        out_shape=shape(2 * RING, 2 * RING, width, width),
        scratch_shapes=[operand_scratch(width)],
        compiler_params=PARAMS,
        name="galerkin_rows",
    )(*tables, slots, here, operator, rows, received, low, high)


def add(terms):
    total = terms[0].astype(jnp.float32)
    for term in terms[1:]:
        total = total + term.astype(jnp.float32)
    return total.astype(jnp.bfloat16)


def body(
    operator_blocks,
    local_columns,
    remote_columns,
    match_slots,
    tentative,
    inverse_diagonal,
    peer,
    slab,
    coarse_slots,
):
    tables = (local_columns.T, remote_columns.T, match_slots.transpose(1, 2, 0))
    slots = coarse_slots.transpose(1, 2, 0)
    here = jnp.stack([lax.axis_index("x"), lax.axis_index("y"), lax.axis_index("c")]).astype(jnp.int32)
    rows = tentative
    up, down = pick(slab, rows)
    low, high = shifted(up, "gx", 1), shifted(down, "gx", -1)
    outgoing = pack(peer, rows)
    outgoing, low, high, here = lax.optimization_barrier((outgoing, low, high, here))
    received = lax.all_to_all(outgoing, GY, split_axis=0, concat_axis=0, tiled=True)
    for smooth_pass in range(2):
        operands = (operator_blocks, inverse_diagonal, rows, received, low, high)
        up, down = slab_rows(tables, slab, *operands)
        up, down, operands = lax.optimization_barrier((up, down, operands))
        low, high = shifted(up, "gx", 1), shifted(down, "gx", -1)
        rows, outgoing = smooth(tables, peer, *operands)
        outgoing, low, high = lax.optimization_barrier((outgoing, low, high))
        received = lax.all_to_all(outgoing, GY, split_axis=0, concat_axis=0, tiled=True)
    sums = galerkin(tables, slots, here, operator_blocks, rows, received, low, high)
    others = [lax.ppermute(sums[RING + j], "c", [(0, 1), (1, 0)]) for j in range(RING)]
    parts = [None] * RING
    ready = None
    for j in (2, 1, 3, 0):
        other = others[j]
        if ready is not None:
            other, parts[ready] = lax.optimization_barrier((other, parts[ready]))
        parts[j] = add((sums[j], other))
        ready = j
    for swapped in range(2):
        terms = [parts[0], *[around(parts[s], s, swapped) for s in range(1, RING)]]
        group = max(terms[0].shape[0] // RING, 2)
        parts = [add([term[j : j + group] for term in terms]) for j in range(0, terms[0].shape[0], group)]
        parts = lax.optimization_barrier(parts)
    total = parts[0]
    core = lax.axis_index("c") == 0
    mine = jnp.where(core, total[:1], total[1:])
    theirs = lax.ppermute(jnp.where(core, total[1:], total[:1]), "c", [(0, 1), (1, 0)])
    first, second = jnp.where(core, mine, theirs), jnp.where(core, theirs, mine)
    return (rows, jnp.concatenate([first, second], axis=0))


def solution(mesh):
    fine = Mesh(mesh.devices.reshape(4, 4, 4, 2), AXES)
    placed = tuple(P(AXES, *[None] * extra) for extra in (3, 1, 1, 2, 3, 2, 1, 1, 2))
    return jax.shard_map(
        body,
        mesh=fine,
        in_specs=placed,
        out_specs=(P(AXES, None, None, None), P(AXES, None, None)),
        check_vma=False,
    )
```

```python
import jax
import jax.numpy as jnp
from jax import lax
from jax.experimental import pallas as pl
from jax.experimental.pallas import tpu as pltpu
from jax.sharding import Mesh
from jax.sharding import PartitionSpec as P

AXES = ("gx", "x", "y", "c")
GY = ("x", "y", "c")
LINKS = 6
LOCAL = 2
BLOCKS = 2
RING = 4
ANY = pl.BlockSpec(memory_space=pl.ANY)
VMEM = pl.BlockSpec(memory_space=pltpu.VMEM)
SMEM = pl.BlockSpec(memory_space=pltpu.SMEM)
PARAMS = pltpu.CompilerParams(vmem_limit_bytes=26 << 20)


def shifted(value, axis, steps):
    count = lax.axis_size(axis)
    first, last = (max(0, -steps), min(count, count - steps))
    return lax.ppermute(value, axis, [(source, source + steps) for source in range(first, last)])


def around(value, steps, swapped):
    pairs = []
    for x in range(RING):
        for y in range(RING):
            for c in range(2):
                to_x, to_y = ((x + steps) % RING, y) if c == swapped else (x, (y + steps) % RING)
                pairs.append(((x * RING + y) * 2 + c, (to_x * RING + to_y) * 2 + c))
    return lax.ppermute(value, GY, pairs)


def shape(*sizes):
    return jax.ShapeDtypeStruct(sizes, jnp.bfloat16)


def pick_kernel(slab, rows_ref, up_ref, down_ref, held, sems):
    arrivals = [pltpu.make_async_copy(rows_ref.at[slab[0, j]], held.at[j], sems.at[j]) for j in range(2)]
    copies = [pltpu.make_async_copy(held.at[j], out.at[0], sems.at[2 + j]) for j, out in enumerate((up_ref, down_ref))]
    for copy in arrivals:
        copy.start()
    for arrival, copy in zip(arrivals, copies):
        arrival.wait()
        copy.start()
    for copy in copies:
        copy.wait()


def pick(slab, rows):
    one = shape(1, *rows.shape[1:])
    return pl.pallas_call(
        pick_kernel,
        in_specs=[SMEM, ANY],
        out_specs=[ANY, ANY],
        out_shape=(one, one),
        scratch_shapes=[pltpu.VMEM((2, *rows.shape[1:]), jnp.bfloat16), pltpu.SemaphoreType.DMA((4,))],
        compiler_params=pltpu.CompilerParams(vmem_limit_bytes=56 << 20),
        name="pick_rows",
    )(slab, rows)


def pack_kernel(peer, rows_ref, out_ref, own, in_sems, sems):
    arrivals = [pltpu.make_async_copy(rows_ref.at[j], own.at[j], in_sems.at[j]) for j in range(own.shape[0])]
    for copy in arrivals:
        copy.start()
    for copy in arrivals:
        copy.wait()
    copies = [pltpu.make_async_copy(own.at[peer[0, q]], out_ref.at[q], sems.at[q]) for q in range(out_ref.shape[0])]
    for copy in copies:
        copy.start()
    for copy in copies:
        copy.wait()


def pack(peer, rows):
    peers = peer.shape[1]
    return pl.pallas_call(
        pack_kernel,
        in_specs=[SMEM, ANY],
        out_specs=ANY,
        out_shape=shape(peers, *rows.shape[1:]),
        scratch_shapes=[
            pltpu.VMEM(rows.shape, jnp.bfloat16),
            pltpu.SemaphoreType.DMA((rows.shape[0],)),
            pltpu.SemaphoreType.DMA((peers,)),
        ],
        cost_estimate=pl.CostEstimate(flops=0, transcendentals=0, bytes_accessed=10 << 20),
        compiler_params=PARAMS,
        name="pack_rows",
    )(peer, rows)


def row_image(local, remote, match, i, a_buf, own, peers, low, high, rhs):
    width = own.shape[-1]
    first, count = own.shape[0], peers.shape[0]
    for k in range(LINKS):
        for n in range(BLOCKS):
            wanted = match[k, n, i]
            there = jnp.minimum(wanted, BLOCKS - 1)
            if k < LOCAL:
                block = own[local[k, i], there]
            else:
                column = remote[k - LOCAL, i]
                block = peers[jnp.clip(column - first, 0, count - 1), there]
                block = jnp.where(column == first + count, low[0, there], block)
                block = jnp.where(column > first + count, high[0, there], block)
            block = jnp.where(wanted < BLOCKS, block, jnp.zeros_like(block))
            rhs[k * width : (k + 1) * width, n * width : (n + 1) * width] = block
    lhs = jnp.concatenate([a_buf[i, k] for k in range(LINKS)], axis=1)
    return jnp.dot(lhs, rhs[...], preferred_element_type=jnp.float32).astype(jnp.bfloat16)


def new_row(local, remote, match, i, a_buf, d_buf, own, peers, low, high, rhs):
    width = own.shape[-1]
    image = row_image(local, remote, match, i, a_buf, own, peers, low, high, rhs)
    update = jnp.dot(d_buf[i], image, preferred_element_type=jnp.float32)
    halves = [update[:, n * width : (n + 1) * width] for n in range(BLOCKS)]
    return [(own[i, n].astype(jnp.float32) - halves[n]).astype(jnp.bfloat16) for n in range(BLOCKS)]


def slab_kernel(
    local, remote, match, slab,
    a_buf, d_buf, own, peers, low, high,
    up, down,
    rhs,
):
    for j, out in enumerate((up, down)):
        for n, value in enumerate(new_row(local, remote, match, slab[0, j], a_buf, d_buf, own, peers, low, high, rhs.at[j])):
            out[0, n] = value


def smooth_kernel(
    local, remote, match, peer,
    a_buf, d_buf, own, peers, low, high,
    rows_hbm, out_hbm,
    new, rhs,
    rows_sem, out_sems,
):
    @pl.loop(0, own.shape[0], step=4)
    def _(start):
        for lane in range(4):
            i = start + lane
            for n, value in enumerate(new_row(local, remote, match, i, a_buf, d_buf, own, peers, low, high, rhs.at[lane])):
                new[i, n] = value
        for lane in range(4):
            pltpu.make_async_copy(new.at[start + lane], rows_hbm.at[start + lane], rows_sem.at[0]).start()

    copies = [pltpu.make_async_copy(new.at[peer[0, q]], out_hbm.at[q], out_sems.at[q]) for q in range(out_hbm.shape[0])]
    for copy in copies:
        copy.start()
    pltpu.make_async_copy(rows_hbm, rows_hbm, rows_sem.at[0]).wait()
    for copy in copies:
        copy.wait()


def operand_scratch(width):
    return pltpu.VMEM((4, LINKS * width, BLOCKS * width), jnp.bfloat16)


def slab_rows(tables, slab, operator, inverse, rows, received, low, high):
    width = operator.shape[-1]
    one = shape(1, *rows.shape[1:])
    return pl.pallas_call(
        slab_kernel,
        in_specs=[SMEM] * 4 + [VMEM] * 6,
        out_specs=[VMEM] * 2,
        out_shape=(one, one),
        scratch_shapes=[operand_scratch(width)],
        compiler_params=PARAMS,
        name="slab_rows",
    )(*tables, slab, operator, inverse, rows, received, low, high)


def smooth(tables, peer, operator, inverse, rows, received, low, high):
    count, _, width, _ = operator.shape
    flops = 2 * count * (LINKS + 1) * BLOCKS * width**3
    return pl.pallas_call(
        smooth_kernel,
        in_specs=[SMEM] * 4 + [VMEM] * 6,
        out_specs=[ANY, ANY],
        out_shape=(shape(*rows.shape), shape(*received.shape)),
        scratch_shapes=[
            pltpu.VMEM(rows.shape, jnp.bfloat16),
            operand_scratch(width),
            pltpu.SemaphoreType.DMA((1,)),
            pltpu.SemaphoreType.DMA((received.shape[0],)),
        ],
        cost_estimate=pl.CostEstimate(flops=flops, transcendentals=0, bytes_accessed=28 << 20),
        compiler_params=PARAMS,
        name="smooth_rows",
    )(*tables, peer, operator, inverse, rows, received, low, high)


def galerkin_kernel(
    local, remote, match, slots, here,
    a_buf, own, peers, low, high,
    sums,
    rhs,
):
    width = own.shape[-1]
    sums[...] = jnp.zeros_like(sums)

    @pl.loop(0, own.shape[0], step=4)
    def _(start):
        for lane in range(4):
            i = start + lane
            image = row_image(local, remote, match, i, a_buf, own, peers, low, high, rhs.at[lane])
            mine = jnp.concatenate([own[i, n] for n in range(BLOCKS)], axis=1)
            partial = lax.dot_general(mine, image, (((0,), (0,)), ((), ())), preferred_element_type=jnp.float32)
            for n1 in range(BLOCKS):
                for n2 in range(BLOCKS):
                    slot = slots[n1, n2, i]
                    owner = slot // 2
                    chip = owner // 2
                    dx = (chip // RING - here[0] + RING) % RING
                    dy = (chip % RING - here[1] + RING) % RING
                    second = slot % 2
                    step = jnp.where(second == 0, dx, dy)
                    place = jnp.where(second == 0, dy, dx) * 2 + owner % 2
                    group = jnp.where(second == here[2], 0, RING) + step
                    block = partial[n1 * width : (n1 + 1) * width, n2 * width : (n2 + 1) * width]
                    sums[group, place] = block.astype(jnp.bfloat16)


def galerkin(tables, slots, here, operator, rows, received, low, high):
    width = operator.shape[-1]
    return pl.pallas_call(
        galerkin_kernel,
        in_specs=[SMEM] * 5 + [VMEM] * 5,
        out_specs=VMEM,
        out_shape=shape(2 * RING, 2 * RING, width, width),
        scratch_shapes=[operand_scratch(width)],
        compiler_params=PARAMS,
        name="galerkin_rows",
    )(*tables, slots, here, operator, rows, received, low, high)


def add(terms):
    total = terms[0].astype(jnp.float32)
    for term in terms[1:]:
        total = total + term.astype(jnp.float32)
    return total.astype(jnp.bfloat16)


def body(
    operator_blocks,
    local_columns,
    remote_columns,
    match_slots,
    tentative,
    inverse_diagonal,
    peer,
    slab,
    coarse_slots,
):
    tables = (local_columns.T, remote_columns.T, match_slots.transpose(1, 2, 0))
    slots = coarse_slots.transpose(1, 2, 0)
    here = jnp.stack([lax.axis_index("x"), lax.axis_index("y"), lax.axis_index("c")]).astype(jnp.int32)
    rows = tentative
    up, down = pick(slab, rows)
    low, high = shifted(up, "gx", 1), shifted(down, "gx", -1)
    outgoing = pack(peer, rows)
    outgoing, low, high, here = lax.optimization_barrier((outgoing, low, high, here))
    received = lax.all_to_all(outgoing, GY, split_axis=0, concat_axis=0, tiled=True)
    for smooth_pass in range(2):
        operands = (operator_blocks, inverse_diagonal, rows, received, low, high)
        up, down = slab_rows(tables, slab, *operands)
        up, down, operands = lax.optimization_barrier((up, down, operands))
        low, high = shifted(up, "gx", 1), shifted(down, "gx", -1)
        rows, outgoing = smooth(tables, peer, *operands)
        outgoing, low, high = lax.optimization_barrier((outgoing, low, high))
        received = lax.all_to_all(outgoing, GY, split_axis=0, concat_axis=0, tiled=True)
    sums = galerkin(tables, slots, here, operator_blocks, rows, received, low, high)
    others = [lax.ppermute(sums[RING + j], "c", [(0, 1), (1, 0)]) for j in range(RING)]
    parts = [None] * RING
    ready = None
    for j in (2, 1, 3, 0):
        other = others[j]
        if ready is not None:
            other, parts[ready] = lax.optimization_barrier((other, parts[ready]))
        parts[j] = add((sums[j], other))
        ready = j
    for swapped in range(2):
        terms = [parts[0], *[around(parts[s], s, swapped) for s in range(1, RING)]]
        group = max(terms[0].shape[0] // RING, 2)
        parts = [add([term[j : j + group] for term in terms]) for j in range(0, terms[0].shape[0], group)]
        parts = lax.optimization_barrier(parts)
    total = parts[0]
    core = lax.axis_index("c") == 0
    mine = jnp.where(core, total[:1], total[1:])
    theirs = lax.ppermute(jnp.where(core, total[1:], total[:1]), "c", [(0, 1), (1, 0)])
    first, second = jnp.where(core, mine, theirs), jnp.where(core, theirs, mine)
    return (rows, jnp.concatenate([first, second], axis=0))


def solution(mesh):
    fine = Mesh(mesh.devices.reshape(4, 4, 4, 2), AXES)
    placed = tuple(P(AXES, *[None] * extra) for extra in (3, 1, 1, 2, 3, 2, 1, 1, 2))
    return jax.shard_map(
        body,
        mesh=fine,
        in_specs=placed,
        out_specs=(P(AXES, None, None, None), P(AXES, None, None)),
        check_vma=False,
    )
```
